32 devices in a mesh: section: 2 (over x), dp: 16 (over z, y, core).
Axes of the slice: x: 2, y: 2, z: 4, core: 2. Of those that a mesh axis runs over, the one named last changes fastest.
Arguments:
- residual_in: bfloat16 [2048, 4096], P('dp'), may hold values from -4 to 4
- cotangent: bfloat16 [2048, 4096], P('dp'), may hold values from -4 to 4
- norm_gain: bfloat16 [2, 4096], P('section'), may hold values from 0.25 to 1.75
- value_blocks: bfloat16 [2, 64, 128, 128], P('section', 'dp'), may hold values from -0.1875 to 0.1875
- output_blocks: bfloat16 [2, 256, 128, 128], P('section', 'dp'), may hold values from -0.1875 to 0.1875
- value_index: int32 [2, 64], P('section'), may hold values from 0 to 255, as said below
- output_index: int32 [2, 256], P('section'), may hold values from 0 to 1023, as said below
- value_count: int32 [2], P('section'), may hold values from 8 to 64, as said below
- output_count: int32 [2], P('section'), may hold values from 32 to 256, as said below
Outputs:
- section_out: bfloat16 [2, 2048, 4096], P('section', 'dp')
- section_grad: bfloat16 [2, 2048, 4096], P('section', 'dp')
- value_grad: float32 [2, 64, 128, 128], P('section', 'dp')
The draws below stay inside these ranges and needn't reach their ends.
Inputs may be any that keep to these rules, and one draw needn't show every extreme that they name: `value_index`: within each layer the 64 entries are distinct; an entry e names row block e // 8 and column block e % (8) of the value projection. `output_index`: within each layer the 256 entries are distinct; an entry e names row block e // 32 and column block e % (32) of the output projection. `value_count`: slots below a layer's count hold its nonzero blocks; some layer uses all 64 slots. `output_count`: slots below a layer's count hold its nonzero blocks; some layer uses all 256 slots.
All inputs are finite; a program needn't handle non-finite values.
Results may differ from the reference program's by a relative error of at most 0.0061.
Values may be sent and summed in bfloat16 or wider, within the bound.
A program may use at most 64 MiB of HBM per device.

```python
import jax
import jax.numpy as jnp
from jax import lax

D = 4096
KVW = 1024
HQW = 4096
BLK = 128
TOK_DEV = 128
TOKENS = 2048
VCAP = 64
OCAP = 256
N_SECTION = 2


def pick_one(sub_key, total_blocks, capacity):
    first_key, second_key = jax.random.split(sub_key)
    others = jax.random.permutation(first_key, total_blocks - 1)[:capacity - 1]
    joined = jnp.concatenate([jnp.full((1,), total_blocks - 1, jnp.int32), others.astype(jnp.int32)])
    return jax.random.permutation(second_key, joined)


def pick_blocks(key, total_blocks, capacity):
    section_keys = jax.random.split(key, N_SECTION)
    chosen = jax.vmap(lambda sub_key: pick_one(sub_key, total_blocks, capacity))(section_keys)
    return chosen.astype(jnp.int32)


def section_counts(key, capacity):
    first_key, second_key = jax.random.split(key)
    counts = jax.random.randint(first_key, (N_SECTION,), capacity // 8, capacity + 1)
    busiest = jax.random.randint(second_key, (), 0, N_SECTION)
    section_order = jnp.arange(N_SECTION)
    counts = jnp.where(section_order == busiest, capacity, counts)
    return counts.astype(jnp.int32)


def draw_value_index(key, part):
    return pick_blocks(jax.random.fold_in(key, 101), D // BLK * (KVW // BLK), VCAP)


def draw_output_index(key, part):
    return pick_blocks(jax.random.fold_in(key, 202), HQW // BLK * (D // BLK), OCAP)


def draw_value_count(key, part):
    return section_counts(jax.random.fold_in(key, 303), VCAP)


def draw_output_count(key, part):
    return section_counts(jax.random.fold_in(key, 404), OCAP)


def block_scale(own_key, shape, pieces, smallest, largest):
    def one(axis_at, blocks):
        draws = jax.random.uniform(jax.random.fold_in(jax.random.fold_in(own_key, 6), axis_at), (blocks,), jnp.float32, smallest / len(pieces), largest / len(pieces))
        return jnp.repeat(jnp.exp(draws), shape[axis_at] // blocks).reshape((-1,) + (1,) * (len(shape) - axis_at - 1))

    level = one(*pieces[0])
    for cut in pieces[1:]:
        level = level * one(*cut)
    return level


def normal_values(key, extent, width, reach, cuts=(), kind=jnp.bfloat16):
    array = width * jax.random.normal(key, extent, jnp.float32)
    if cuts:
        array = array * block_scale(key, extent, cuts, -0.22, 0.18)
    return jnp.clip(array, -reach, reach).astype(kind)


def setup_inputs(seed: int = 0) -> dict:
    key_of = jax.random.split(jax.random.key(seed), 10)
    residual_in = normal_values(key_of[0], (TOKENS, D), 1.0, 4.0, ((0, 16),))
    cotangent = normal_values(key_of[1], (TOKENS, D), 1.0, 4.0, ((0, 16),))
    norm_gain = jnp.clip(1.0 + 0.15 * jax.random.normal(key_of[2], (N_SECTION, D), jnp.float32), 0.25, 1.75).astype(jnp.bfloat16)
    value_blocks = normal_values(key_of[3], (N_SECTION, VCAP, BLK, BLK), (D // 4) ** -0.5, 0.1875, ((0, 2), (1, 16)))
    output_blocks = normal_values(key_of[4], (N_SECTION, OCAP, BLK, BLK), (HQW // 4) ** -0.5, 0.1875, ((0, 2), (1, 16)))
    value_index = draw_value_index(jax.random.fold_in(key_of[9], 71), 0)
    output_index = draw_output_index(jax.random.fold_in(key_of[9], 71), 0)
    value_count = draw_value_count(jax.random.fold_in(key_of[9], 71), 0)
    output_count = draw_output_count(jax.random.fold_in(key_of[9], 71), 0)
    return {"residual_in": residual_in, "cotangent": cotangent, "norm_gain": norm_gain, "value_blocks": value_blocks, "output_blocks": output_blocks, "value_index": value_index, "output_index": output_index, "value_count": value_count, "output_count": output_count}


slot_group = 16
epsilon = 1e-05

def apply_blocks(inputs, packed, read_index, write_index, live_mask, out_blocks, pattern):
    height = inputs.shape[0]
    running = jnp.zeros((height, out_blocks, packed.shape[-1]), jnp.float32)

    def one_turn(turn_index, running):
        offset = (turn_index * slot_group).astype(jnp.int32)
        chosen = lax.dynamic_slice_in_dim(packed, offset, slot_group, 0)
        reading = lax.dynamic_slice_in_dim(read_index, offset, slot_group, 0)
        writing = lax.dynamic_slice_in_dim(write_index, offset, slot_group, 0)
        keeping = lax.dynamic_slice_in_dim(live_mask, offset, slot_group, 0)
        picked = jnp.take(inputs, reading, axis=1).astype(jnp.float32)
        product = jnp.einsum(pattern, picked, chosen.astype(jnp.float32))
        return running.at[:, writing, :].add(product * keeping[None, :, None])
    return lax.fori_loop(0, packed.shape[0] // slot_group, one_turn, running)

def reference(residual_in, cotangent, norm_gain, value_blocks, output_blocks, value_index, output_index, value_count, output_count):
    token_count = residual_in.shape[0]
    row_blocks = D // BLK
    head_blocks = KVW // BLK
    group_size = HQW // KVW
    value_slots = jnp.arange(VCAP)
    output_slots = jnp.arange(OCAP)
    current = residual_in
    saved_inputs = []
    saved_normed = []
    outputs = []
    for layer_index in range(N_SECTION):
        value_from = value_index[layer_index] // head_blocks
        value_to = value_index[layer_index] % head_blocks
        output_from = output_index[layer_index] // row_blocks // group_size
        output_to = output_index[layer_index] % row_blocks
        value_live = (value_slots < value_count[layer_index]).astype(jnp.float32)
        output_live = (output_slots < output_count[layer_index]).astype(jnp.float32)
        wide_input = current.astype(jnp.float32)
        scale_row = lax.rsqrt(lax.optimization_barrier(jnp.mean(wide_input * wide_input, axis=-1, keepdims=True)) + epsilon)
        normed = (wide_input * scale_row * norm_gain[layer_index].astype(jnp.float32)).astype(jnp.bfloat16)
        values = apply_blocks(normed.reshape(token_count, row_blocks, BLK), value_blocks[layer_index], value_from, value_to, value_live, head_blocks, 'tgk,gkn->tgn')
        values = values.reshape(token_count, KVW).astype(jnp.bfloat16)
        mixed = apply_blocks(values.reshape(token_count, head_blocks, BLK), output_blocks[layer_index], output_from, output_to, output_live, row_blocks, 'tgk,gkn->tgn')
        saved_inputs.append(current)
        saved_normed.append(normed)
        current = (wide_input + mixed.reshape(token_count, D)).astype(jnp.bfloat16)
        outputs.append(current)
    arriving = cotangent
    gradients = [None] * N_SECTION
    value_grads = [None] * N_SECTION
    for layer_index in reversed(range(N_SECTION)):
        value_from = value_index[layer_index] // head_blocks
        value_to = value_index[layer_index] % head_blocks
        output_from = output_index[layer_index] // row_blocks // group_size
        output_to = output_index[layer_index] % row_blocks
        value_live = (value_slots < value_count[layer_index]).astype(jnp.float32)
        output_live = (output_slots < output_count[layer_index]).astype(jnp.float32)
        grad_wide = arriving.astype(jnp.float32)
        grad_value = apply_blocks(arriving.reshape(token_count, row_blocks, BLK), output_blocks[layer_index], output_to, output_from, output_live, head_blocks, 'tgn,gkn->tgk')
        grad_value = grad_value.reshape(token_count, KVW).astype(jnp.bfloat16)
        normed_grad = apply_blocks(grad_value.reshape(token_count, head_blocks, BLK), value_blocks[layer_index], value_to, value_from, value_live, row_blocks, 'tgn,gkn->tgk')
        normed_grad = normed_grad.reshape(token_count, D)
        wide_input = saved_inputs[layer_index].astype(jnp.float32)
        scale_row = lax.rsqrt(lax.optimization_barrier(jnp.mean(wide_input * wide_input, axis=-1, keepdims=True)) + epsilon)
        gained = normed_grad * norm_gain[layer_index].astype(jnp.float32)
        inner_mean = lax.optimization_barrier(jnp.mean(gained * wide_input, axis=-1, keepdims=True))
        input_grad = grad_wide + scale_row * gained - scale_row * scale_row * scale_row * wide_input * inner_mean
        gradients[layer_index] = input_grad.astype(jnp.bfloat16)
        picked_in = jnp.take(saved_normed[layer_index].reshape(token_count, row_blocks, BLK), value_from, axis=1).astype(jnp.float32)
        picked_out = jnp.take(grad_value.reshape(token_count, head_blocks, BLK), value_to, axis=1).astype(jnp.float32)
        partial_sum = jnp.einsum('tgk,tgn->gkn', picked_in, picked_out)
        value_grads[layer_index] = partial_sum * (value_live / TOK_DEV)[:, None, None]
        arriving = gradients[layer_index]
    return (jnp.stack(outputs), jnp.stack(gradients), jnp.stack(value_grads))
```

```python
import functools

import jax
import jax.numpy as jnp
from jax import lax
from jax.experimental import pallas as pl
from jax.experimental.pallas import tpu as pltpu
from jax.sharding import PartitionSpec as P

KVW = 1024
HQW = 4096
EPS = 1e-05
BF = jnp.bfloat16
F32 = jnp.float32
ROWS = 16
NN = (((1,), (0,)), ((), ()))
NT = (((1,), (1,)), ((), ()))
VMEM = pl.BlockSpec(memory_space=pltpu.VMEM)
SMEM = pl.BlockSpec(memory_space=pltpu.SMEM)


def dot(a, b, dims):
    return lax.dot_general(a, b, dims, preferred_element_type=F32)


def tile(i, n):
    return pl.ds(pl.multiple_of(i * n, n), n)


def loop(n, body):
    def step(i, c):
        body(i)
        return c

    lax.fori_loop(0, n, step, 0)


def build_dense(meta, vidx, oidx, vp, op, wv, we, acc):
    blk = vp.shape[-1]
    heads = wv.shape[1] // blk
    rows = we.shape[1] // blk
    group = HQW // KVW

    def zero_v(i):
        wv[tile(i, blk), :] = jnp.zeros((blk, wv.shape[1]), BF)

    loop(wv.shape[0] // blk, zero_v)

    def zero_a(i):
        acc[tile(i, 32), :] = jnp.zeros((32, acc.shape[1]), F32)

    loop(acc.shape[0] // 32, zero_a)

    def put_v(j):
        e = vidx[0, j]
        wv[tile(lax.div(e, heads), blk), tile(lax.rem(e, heads), blk)] = vp[j]

    loop(meta[1], put_v)

    def put_o(j):
        e = oidx[0, j]
        r = tile(lax.div(e, rows * group), blk)
        c = tile(lax.rem(e, rows), blk)
        acc[r, c] += op[j].astype(F32)

    loop(meta[2], put_o)

    def cast(i):
        we[tile(i, 32), :] = acc[tile(i, 32), :].astype(BF)

    loop(acc.shape[0] // 32, cast)


def norm(x_ref, gain, u_ref):
    def body(i):
        s = tile(i, ROWS)
        x = x_ref[s, :].astype(F32)
        r = lax.rsqrt(jnp.mean(x * x, axis=-1, keepdims=True) + EPS)
        u_ref[s, :] = (x * r * gain[...].astype(F32)).astype(BF)

    loop(x_ref.shape[0] // ROWS, body)


def forward(x_ref, u_ref, wv, we, v_ref, out_ref):
    def values(i):
        c = tile(i, 256)
        v_ref[:, c] = dot(u_ref[...], wv[:, c], NN).astype(BF)

    loop(wv.shape[1] // 256, values)

    def mixed(i):
        c = tile(i, 512)
        m = dot(v_ref[...], we[:, c], NN)
        out_ref[:, c] = (x_ref[:, c].astype(F32) + m).astype(BF)

    loop(we.shape[1] // 512, mixed)


def backward_values(g_ref, we, dv_ref):
    def body(i):
        c = tile(i, 256)
        dv_ref[:, c] = dot(g_ref[...], we[c, :], NT).astype(BF)

    loop(we.shape[0] // 256, body)


def backward_gained(dv_ref, wv, gain, e_refs):
    def body(i):
        c = tile(i, 512)
        e = dot(dv_ref[...], wv[c, :], NT) * gain[:, c].astype(F32)
        for ref in e_refs:
            ref[:, c] = e.astype(ref.dtype)

    loop(wv.shape[0] // 512, body)


def backward_norm(g_ref, x_ref, e_ref, out_ref):
    def body(i):
        s = tile(i, ROWS)
        x = x_ref[s, :].astype(F32)
        e = e_ref[s, :].astype(F32)
        r = lax.rsqrt(jnp.mean(x * x, axis=-1, keepdims=True) + EPS)
        m = jnp.mean(e * x, axis=-1, keepdims=True)
        out_ref[s, :] = (g_ref[s, :].astype(F32) + r * e - (r * r * r * m) * x).astype(BF)

    loop(x_ref.shape[0] // ROWS, body)


def slot_grads(meta, vidx, u_ref, dv_ref, ut_ref, part_ref):
    tokens = u_ref.shape[0]
    slots, blk = part_ref.shape[0], part_ref.shape[-1]
    heads = dv_ref.shape[1] // blk

    def flip(i):
        ut_ref[tile(i, blk), :] = u_ref[:, tile(i, blk)].T

    loop(u_ref.shape[1] // blk, flip)

    def body(j):
        e = vidx[0, j]
        live = jnp.where(j < meta[1], 1.0 / tokens, 0.0)
        p = dot(ut_ref[tile(lax.div(e, heads), blk), :], dv_ref[:, tile(lax.rem(e, heads), blk)], NN)
        part_ref[j] = p * live

    def four(i):
        for k in range(4):
            body(i * 4 + k)

    loop(slots // 4, four)


def first_stage(meta, vidx, oidx, vp, op, x, g, gain, wv, we, send, u, e32, dv, acc, v):
    build_dense(meta, vidx, oidx, vp, op, wv, we, acc)

    @pl.when(meta[0] == 0)
    def _():
        norm(x, gain, u)
        forward(x, u, wv, we, v, send)

    @pl.when(meta[0] == 1)
    def _():
        backward_values(g, we, dv)
        backward_gained(dv, wv, gain, (send, e32))


def second_stage(meta, vidx, wv, we, x, g, gain, sent, got, u, e32, dv, out, grad, part, v, g1, u2, dv2, ut):
    @pl.when(meta[0] == 0)
    def _():
        out[...] = sent[...]
        backward_norm(g, sent, got, g1)
        backward_values(g1, we, dv2)
        backward_gained(dv2, wv, gain, (e32,))
        backward_norm(g1, x, e32, grad)
        slot_grads(meta, vidx, u, dv2, ut, part)

    @pl.when(meta[0] == 1)
    def _():
        backward_norm(g, got, e32, grad)
        norm(got, gain, u2)
        forward(got, u2, wv, we, v, out)
        slot_grads(meta, vidx, u2, dv, ut, part)


def params():
    return pltpu.CompilerParams(vmem_limit_bytes=62 << 20)


def cost(flops, data):
    return pl.CostEstimate(flops=flops, bytes_accessed=data, transcendentals=0)


def scatter_grads(part):
    return lax.psum_scatter(part, "dp", scatter_dimension=0, tiled=True)


def two_sections(meta, vidx, oidx, vp, op, x, g, gain):
    tokens, width = x.shape
    slots, blk, _ = vp.shape
    wide = jax.ShapeDtypeStruct((tokens, width), BF)
    narrow = jax.ShapeDtypeStruct((tokens, KVW), BF)
    wide32 = jax.ShapeDtypeStruct((tokens, width), F32)
    wv, we, send, u, e32, dv = pl.pallas_call(
        first_stage,
        out_shape=(
            jax.ShapeDtypeStruct((width, KVW), BF),
            jax.ShapeDtypeStruct((KVW, width), BF),
            wide,
            wide,
            wide32,
            narrow,
        ),
        in_specs=[SMEM] * 3 + [VMEM] * 5,
        out_specs=(VMEM,) * 6,
        scratch_shapes=[pltpu.VMEM((KVW, width), F32), pltpu.VMEM((tokens, KVW), BF)],
        compiler_params=params(),
        name="first_stage",
    )(meta, vidx, oidx, vp, op, x, g, gain)
    got = lax.ppermute(send, "section", [(0, 1), (1, 0)])
    out, grad, part = pl.pallas_call(
        second_stage,
        out_shape=(wide, wide, jax.ShapeDtypeStruct((slots, blk, blk), F32)),
        in_specs=[SMEM] * 2 + [VMEM] * 10,
        out_specs=(VMEM,) * 3,
        scratch_shapes=[
            pltpu.VMEM((tokens, KVW), BF),
            pltpu.VMEM((tokens, width), BF),
            pltpu.VMEM((tokens, width), BF),
            pltpu.VMEM((tokens, KVW), BF),
            pltpu.VMEM((width, tokens), BF),
        ],
        compiler_params=params(),
        name="second_stage",
    )(meta, vidx, wv, we, x, g, gain, send, got, u, e32, dv)
    return out, grad, part


def many_sections(meta, vidx, oidx, vp, op, x, g, gain):
    sections = lax.axis_size("section")
    here = meta[0]
    tokens, width = x.shape
    slots, blk, _ = vp.shape
    wv, we = pl.pallas_call(
        build_dense,
        out_shape=(jax.ShapeDtypeStruct((width, KVW), BF), jax.ShapeDtypeStruct((KVW, width), BF)),
        in_specs=[SMEM] * 3 + [VMEM] * 2,
        out_specs=(VMEM,) * 2,
        scratch_shapes=[pltpu.VMEM((KVW, width), F32)],
        compiler_params=params(),
        name="build_dense",
    )(meta, vidx, oidx, vp, op)
    gain_row = gain.astype(F32)

    def scale(a):
        return lax.rsqrt(jnp.mean(a * a, axis=-1, keepdims=True) + EPS)

    def layer(cur):
        a = cur.astype(F32)
        u = (a * scale(a) * gain_row).astype(BF)
        v = dot(u, wv, NN).astype(BF)
        return (a + dot(v, we, NN)).astype(BF), u

    def fwd(t, cur):
        got = lax.ppermute(layer(cur)[0], "section", [(i, i + 1) for i in range(sections - 1)])
        return jnp.where(here == t + 1, got, cur)

    cur = lax.fori_loop(0, sections - 1, fwd, x)
    out, u = layer(cur)
    a = cur.astype(F32)
    r = scale(a)

    def back(gin):
        dv = dot(gin, we, NT).astype(BF)
        e = dot(dv, wv, NT) * gain_row
        m = jnp.mean(e * a, axis=-1, keepdims=True)
        return (gin.astype(F32) + r * e - r * r * r * a * m).astype(BF), dv

    def bwd(t, gin):
        got = lax.ppermute(back(gin)[0], "section", [(i + 1, i) for i in range(sections - 1)])
        return jnp.where(here == sections - 2 - t, got, gin)

    gin = lax.fori_loop(0, sections - 1, bwd, g)
    grad, dv = back(gin)
    heads = KVW // blk
    picked_in = jnp.take(u.reshape(tokens, -1, blk), vidx[0] // heads, axis=1)
    picked_out = jnp.take(dv.reshape(tokens, heads, blk), vidx[0] % heads, axis=1)
    part = jnp.einsum("tgk,tgn->gkn", picked_in, picked_out, preferred_element_type=F32)
    live = (jnp.arange(slots) < meta[1]).astype(F32) / tokens
    return out, grad, part * live[:, None, None]


def on_device(x, g, gain, value_blocks, output_blocks, vidx, oidx, vcount, ocount):
    sections = lax.axis_size("section")
    here = lax.axis_index("section").astype(jnp.int32)
    vp = lax.all_gather(value_blocks[0], "dp", axis=0, tiled=True)
    op = lax.all_gather(output_blocks[0], "dp", axis=0, tiled=True)
    meta = jnp.stack([here, vcount[0], ocount[0]])
    run = two_sections if sections == 2 else many_sections
    out, grad, part = run(meta, vidx, oidx, vp, op, x, g, gain)
    vgrad = scatter_grads(part)
    return out[None], grad[None], vgrad[None]


def solution(mesh):
    return jax.shard_map(
        on_device,
        mesh=mesh,
        in_specs=(
            P("dp", None),
            P("dp", None),
            P("section", None),
            P("section", "dp", None, None),
            P("section", "dp", None, None),
            P("section", None),
            P("section", None),
            P("section"),
            P("section"),
        ),
        out_specs=(
            P("section", "dp", None),
            P("section", "dp", None),
            P("section", "dp", None, None),
        ),
        check_vma=False,
    )
```

```python
import jax
import jax.numpy as jnp
from jax import lax
from jax.experimental import pallas as pl
from jax.experimental.pallas import tpu as pltpu
from jax.sharding import PartitionSpec as P

KVW = 1024
HQW = 4096
EPS = 1e-05
BF = jnp.bfloat16
F32 = jnp.float32
ROWS = 16
NN = (((1,), (0,)), ((), ()))
NT = (((1,), (1,)), ((), ()))
VMEM = pl.BlockSpec(memory_space=pltpu.VMEM)
SMEM = pl.BlockSpec(memory_space=pltpu.SMEM)


def dot(a, b, dims):
    return lax.dot_general(a, b, dims, preferred_element_type=F32)


def tile(i, n):
    return pl.ds(pl.multiple_of(i * n, n), n)


def loop(n, body):
    def step(i, c):
        body(i)
        return c

    lax.fori_loop(0, n, step, 0)


def build_dense(meta, vidx, oidx, vp, op, wv, we, acc):
    blk = vp.shape[-1]
    heads = wv.shape[1] // blk
    rows = we.shape[1] // blk
    group = HQW // KVW

    def zero_v(i):
        wv[tile(i, blk), :] = jnp.zeros((blk, wv.shape[1]), BF)

    loop(wv.shape[0] // blk, zero_v)

    def zero_a(i):
        acc[tile(i, 32), :] = jnp.zeros((32, acc.shape[1]), F32)

    loop(acc.shape[0] // 32, zero_a)

    def put_v(j):
        e = vidx[0, j]
        wv[tile(lax.div(e, heads), blk), tile(lax.rem(e, heads), blk)] = vp[j]

    loop(meta[1], put_v)

    def put_o(j):
        e = oidx[0, j]
        r = tile(lax.div(e, rows * group), blk)
        c = tile(lax.rem(e, rows), blk)
        acc[r, c] += op[j].astype(F32)

    loop(meta[2], put_o)

    def cast(i):
        we[tile(i, 32), :] = acc[tile(i, 32), :].astype(BF)

    loop(acc.shape[0] // 32, cast)


def norm(x_ref, gain, u_ref):
    def body(i):
        s = tile(i, ROWS)
        x = x_ref[s, :].astype(F32)
        r = lax.rsqrt(jnp.mean(x * x, axis=-1, keepdims=True) + EPS)
        u_ref[s, :] = (x * r * gain[...].astype(F32)).astype(BF)

    loop(x_ref.shape[0] // ROWS, body)


def forward(x_ref, u_ref, wv, we, v_ref, out_ref):
    def values(i):
        c = tile(i, 256)
        v_ref[:, c] = dot(u_ref[...], wv[:, c], NN).astype(BF)

    loop(wv.shape[1] // 256, values)

    def mixed(i):
        c = tile(i, 512)
        m = dot(v_ref[...], we[:, c], NN)
        out_ref[:, c] = (x_ref[:, c].astype(F32) + m).astype(BF)

    loop(we.shape[1] // 512, mixed)


def backward_values(g_ref, we, dv_ref):
    def body(i):
        c = tile(i, 256)
        dv_ref[:, c] = dot(g_ref[...], we[c, :], NT).astype(BF)

    loop(we.shape[0] // 256, body)


def backward_gained(dv_ref, wv, gain, e_refs):
    def body(i):
        c = tile(i, 512)
        e = dot(dv_ref[...], wv[c, :], NT) * gain[:, c].astype(F32)
        for ref in e_refs:
            ref[:, c] = e.astype(ref.dtype)

    loop(wv.shape[0] // 512, body)


def backward_norm(g_ref, x_ref, e_ref, out_ref):
    def body(i):
        s = tile(i, ROWS)
        x = x_ref[s, :].astype(F32)
        e = e_ref[s, :].astype(F32)
        r = lax.rsqrt(jnp.mean(x * x, axis=-1, keepdims=True) + EPS)
        m = jnp.mean(e * x, axis=-1, keepdims=True)
        out_ref[s, :] = (g_ref[s, :].astype(F32) + r * e - (r * r * r * m) * x).astype(BF)

    loop(x_ref.shape[0] // ROWS, body)


def slot_grads(meta, vidx, u_ref, dv_ref, ut_ref, part_ref):
    tokens = u_ref.shape[0]
    slots, blk = part_ref.shape[0], part_ref.shape[-1]
    heads = dv_ref.shape[1] // blk

    def flip(i):
        ut_ref[tile(i, blk), :] = u_ref[:, tile(i, blk)].T

    loop(u_ref.shape[1] // blk, flip)

    def body(j):
        e = vidx[0, j]
        live = jnp.where(j < meta[1], 1.0 / tokens, 0.0)
        p = dot(ut_ref[tile(lax.div(e, heads), blk), :], dv_ref[:, tile(lax.rem(e, heads), blk)], NN)
        part_ref[j] = p * live

    def four(i):
        for k in range(4):
            body(i * 4 + k)

    loop(slots // 4, four)


def first_stage(meta, vidx, oidx, vp, op, x, g, gain, wv, we, send, u, e32, dv, acc, v):
    build_dense(meta, vidx, oidx, vp, op, wv, we, acc)

    @pl.when(meta[0] == 0)
    def _():
        norm(x, gain, u)
        forward(x, u, wv, we, v, send)

    @pl.when(meta[0] == 1)
    def _():
        backward_values(g, we, dv)
        backward_gained(dv, wv, gain, (send, e32))


def second_stage(meta, vidx, wv, we, x, g, gain, sent, got, u, e32, dv, out, grad, part, v, g1, u2, dv2, ut):
    @pl.when(meta[0] == 0)
    def _():
        out[...] = sent[...]
        backward_norm(g, sent, got, g1)
        backward_values(g1, we, dv2)
        backward_gained(dv2, wv, gain, (e32,))
        backward_norm(g1, x, e32, grad)
        slot_grads(meta, vidx, u, dv2, ut, part)

    @pl.when(meta[0] == 1)
    def _():
        backward_norm(g, got, e32, grad)
        norm(got, gain, u2)
        forward(got, u2, wv, we, v, out)
        slot_grads(meta, vidx, u2, dv, ut, part)


def params():
    return pltpu.CompilerParams(vmem_limit_bytes=62 << 20)


def cost(flops, data):
    return pl.CostEstimate(flops=flops, bytes_accessed=data, transcendentals=0)


class Links:
    def __init__(self):
        me = lax.axis_index("dp")
        self.me = me
        self.z, self.y, self.c = lax.div(me, 4), lax.rem(lax.div(me, 2), 2), lax.rem(me, 2)
        self.up, self.down = me + 4, me - 4
        self.has_up, self.has_down = self.z < 3, self.z > 0
        self.side = me + 2 - 4 * self.y
        self.twin = me + 1 - 2 * self.c

    def greet(self, chain):
        barrier = pltpu.get_barrier_semaphore()

        def hello(dev):
            pl.semaphore_signal(barrier, inc=1, device_id={"dp": dev}, device_id_type=pl.DeviceIdType.MESH)

        hello(self.side)
        hello(self.twin)
        if chain:
            pl.when(self.has_up)(lambda: hello(self.up))
            pl.when(self.has_down)(lambda: hello(self.down))
            pl.semaphore_wait(barrier, 2 + (self.has_up).astype(jnp.int32) + (self.has_down).astype(jnp.int32))
        else:
            for k in range(1, 4):
                hello(lax.rem(self.z + k, 4) * 4 + lax.rem(self.me, 4))
            pl.semaphore_wait(barrier, 5)


def remote(src, dst, send_sem, recv_sem, dev):
    return pltpu.make_async_remote_copy(
        src_ref=src,
        dst_ref=dst,
        send_sem=send_sem,
        recv_sem=recv_sem,
        device_id={"dp": dev},
        device_id_type=pl.DeviceIdType.MESH,
    )


def gather_kernel(v_in, o_in, v_all, o_all, send_sem, recv_sem, own_sem):
    at = Links()
    nv, no = v_in.shape[0], o_in.shape[0]
    half = no // 2
    kinds = ((v_in, v_all, nv, nv, 0), (o_in, o_all, no, half, 0), (o_in, o_all, no, half, half))
    own_v = pltpu.make_async_copy(v_in, v_all.at[pl.ds(at.me * nv, nv)], own_sem.at[0])
    own_o = pltpu.make_async_copy(o_in, o_all.at[pl.ds(at.me * no, no)], own_sem.at[1])
    own_v.start()
    own_o.start()
    at.greet(True)
    started = []

    def place(kind, origin):
        _, ref, stride, size, base = kinds[kind]
        return ref.at[pl.ds(origin * stride + base, size)]

    def send(kind, origin, own, way, dev, when):
        ref, _, _, size, base = kinds[kind]
        src = ref.at[pl.ds(base, size)] if own else place(kind, origin)
        lane = lax.div(origin, 2)
        copy = remote(src, place(kind, origin), send_sem.at[kind, lane, way], recv_sem.at[kind, origin], dev)
        if when is None:
            copy.start()
        else:
            pl.when(when)(copy.start)
        return copy, when

    def wait(kind, origin):
        dst = place(kind, origin)
        remote(dst, dst, send_sem.at[kind, 0, 0], recv_sem.at[kind, origin], at.twin).wait_recv()

    def finish(copy, when):
        if when is None:
            copy.wait_send()
        else:
            pl.when(when)(copy.wait_send)

    for kind in (1, 0, 2):
        started.append(send(kind, at.me, True, 0, at.up, at.has_up))
        started.append(send(kind, at.me, True, 1, at.down, at.has_down))
        started.append(send(kind, at.me, True, 2, at.side, None))
        started.append(send(kind, at.me, True, 3, at.twin, None))
    wait(0, at.side)
    started.append(send(0, at.side, False, 0, at.up, at.has_up))
    started.append(send(0, at.side, False, 1, at.down, at.has_down))
    started.append(send(0, at.side, False, 3, at.twin, None))
    tails = []

    for hop in (1, 2, 3):
        for kind, swap in ((1, False), (0, False), (2, False), (0, True)):
            for sign in (-1, 1):
                far = at.z + sign * hop
                there = (far >= 0) & (far < 4)
                origin = (at.side if swap else at.me) + 4 * sign * hop

                def relay(kind=kind, origin=origin, sign=sign):
                    wait(kind, origin)
                    if sign < 0:
                        send(kind, origin, False, 0, at.up, at.has_up)
                    else:
                        send(kind, origin, False, 1, at.down, at.has_down)
                    if kind > 0:
                        send(kind, origin, False, 2, at.side, None)
                    send(kind, origin, False, 3, at.twin, None)

                def ended(kind=kind, origin=origin, sign=sign):
                    def gone(way, dev):
                        src = place(kind, origin)
                        lane = lax.div(origin, 2)
                        return remote(src, src, send_sem.at[kind, lane, way], recv_sem.at[kind, origin], dev).wait_send

                    if sign < 0:
                        pl.when(at.has_up)(gone(0, at.up))
                    else:
                        pl.when(at.has_down)(gone(1, at.down))
                    if kind > 0:
                        gone(2, at.side)()
                    gone(3, at.twin)()

                pl.when(there)(relay)
                tails.append((there, ended))
        for sign in (-1, 1) if hop > 1 else (0,):
            far = at.z + sign * (hop - 1)
            side_block(at, wait, send, started, tails, far, at.side + 4 * sign * (hop - 1), place, send_sem, recv_sem)
    for sign in (-1, 1):
        side_block(at, wait, send, started, tails, at.z + sign * 3, at.side + 12 * sign, place, send_sem, recv_sem)
    for copy, when in started:
        finish(copy, when)
    for there, ended in tails:
        pl.when(there)(ended)
    for k in range(8):
        for kind in range(3):
            wait(kind, 2 * k + 1 - at.c)
    own_v.wait()
    own_o.wait()


def side_block(at, wait, send, started, tails, far, origin, place, send_sem, recv_sem):
    there = (far >= 0) & (far < 4)

    def relay():
        for kind in (1, 2):
            wait(kind, origin)
            send(kind, origin, False, 3, at.twin, None)

    def ended():
        for kind in (1, 2):
            src = place(kind, origin)
            lane = lax.div(origin, 2)
            remote(src, src, send_sem.at[kind, lane, 3], recv_sem.at[kind, origin], at.twin).wait_send()

    pl.when(there)(relay)
    tails.append((there, ended))


def gather_blocks(value_blocks, output_blocks):
    count = lax.axis_size("dp")
    if count != 16 or lax.axis_size("section") != 2:
        return tuple(lax.all_gather(b, "dp", axis=0, tiled=True) for b in (value_blocks, output_blocks))
    any_space = pl.BlockSpec(memory_space=pl.ANY)

    def whole(b):
        return jax.ShapeDtypeStruct((b.shape[0] * count,) + b.shape[1:], b.dtype)

    return pl.pallas_call(
        gather_kernel,
        out_shape=(whole(value_blocks), whole(output_blocks)),
        in_specs=[any_space] * 2,
        out_specs=(any_space,) * 2,
        scratch_shapes=[
            pltpu.SemaphoreType.DMA((3, 8, 4)),
            pltpu.SemaphoreType.DMA((3, 16)),
            pltpu.SemaphoreType.DMA((2,)),
        ],
        compiler_params=pltpu.CompilerParams(collective_id=0, has_side_effects=True),
        name="gather_blocks",
    )(value_blocks, output_blocks)


def reduce_kernel(part, out, got1, sum1, send2, got2, send3, got3, send_sem, recv_sem):
    at = Links()
    at.greet(False)
    chips, cores, n, blk, _ = part.shape
    first = [
        remote(part.at[k, 1 - at.c], got1.at[k], send_sem.at[k], recv_sem.at[k], at.twin) for k in range(chips)
    ]
    for copy in first:
        copy.start()
    second = []
    for z in range(4):
        for k in (2 * z, 2 * z + 1):
            first[k].wait_recv()
            sum1[k] = part[k, at.c] + got1[k]
        send2[z] = sum1[2 * z + 1 - at.y].astype(BF)
        copy = remote(send2.at[z], got2.at[z], send_sem.at[8 + z], recv_sem.at[8 + z], at.side)
        copy.start()
        second.append(copy)
    for z in range(4):
        second[z].wait_recv()
        k = 2 * z + at.y
        total = sum1[k] + got2[z].astype(F32)
        sum1[k] = total
        send3[z] = total.astype(BF)

        @pl.when(at.z != z)
        def _():
            remote(
                send3.at[z], got3.at[at.z], send_sem.at[12 + z], recv_sem.at[12 + at.z], z * 4 + lax.rem(at.me, 4)
            ).start()

    out[...] = sum1[2 * at.z + at.y]
    for z in range(4):

        @pl.when(at.z != z)
        def _():
            copy = remote(
                send3.at[z], got3.at[z], send_sem.at[12 + z], recv_sem.at[12 + z], z * 4 + lax.rem(at.me, 4)
            )
            copy.wait_recv()
            copy.wait_send()
            out[...] += got3[z].astype(F32)

    for copy in first + second:
        copy.wait_send()


def scatter_grads(part):
    count = lax.axis_size("dp")
    if count != 16 or lax.axis_size("section") != 2:
        return lax.psum_scatter(part, "dp", scatter_dimension=0, tiled=True)
    slots, blk, _ = part.shape
    n = slots // count
    return pl.pallas_call(
        reduce_kernel,
        out_shape=jax.ShapeDtypeStruct((n, blk, blk), F32),
        in_specs=[VMEM],
        out_specs=VMEM,
        scratch_shapes=[
            pltpu.VMEM((8, n, blk, blk), F32),
            pltpu.VMEM((8, n, blk, blk), F32),
            pltpu.VMEM((4, n, blk, blk), BF),
            pltpu.VMEM((4, n, blk, blk), BF),
            pltpu.VMEM((4, n, blk, blk), BF),
            pltpu.VMEM((4, n, blk, blk), BF),
            pltpu.SemaphoreType.DMA((16,)),
            pltpu.SemaphoreType.DMA((16,)),
        ],
        compiler_params=pltpu.CompilerParams(collective_id=1, has_side_effects=True, vmem_limit_bytes=32 << 20),
        name="reduce_grads",
    )(part.reshape(count // 2, 2, n, blk, blk))


def two_sections(meta, vidx, oidx, vp, op, x, g, gain):
    tokens, width = x.shape
    slots, blk, _ = vp.shape
    wide = jax.ShapeDtypeStruct((tokens, width), BF)
    narrow = jax.ShapeDtypeStruct((tokens, KVW), BF)
    wide32 = jax.ShapeDtypeStruct((tokens, width), F32)
    wv, we, send, u, e32, dv = pl.pallas_call(
        first_stage,
        out_shape=(
            jax.ShapeDtypeStruct((width, KVW), BF),
            jax.ShapeDtypeStruct((KVW, width), BF),
            wide,
            wide,
            wide32,
            narrow,
        ),
        in_specs=[SMEM] * 3 + [VMEM] * 5,
        out_specs=(VMEM,) * 6,
        scratch_shapes=[pltpu.VMEM((KVW, width), F32), pltpu.VMEM((tokens, KVW), BF)],
        compiler_params=params(),
        name="first_stage",
    )(meta, vidx, oidx, vp, op, x, g, gain)
    got = lax.ppermute(send, "section", [(0, 1), (1, 0)])
    out, grad, part = pl.pallas_call(
        second_stage,
        out_shape=(wide, wide, jax.ShapeDtypeStruct((slots, blk, blk), F32)),
        in_specs=[SMEM] * 2 + [VMEM] * 10,
        out_specs=(VMEM,) * 3,
        scratch_shapes=[
            pltpu.VMEM((tokens, KVW), BF),
            pltpu.VMEM((tokens, width), BF),
            pltpu.VMEM((tokens, width), BF),
            pltpu.VMEM((tokens, KVW), BF),
            pltpu.VMEM((width, tokens), BF),
        ],
        compiler_params=params(),
        name="second_stage",
    )(meta, vidx, wv, we, x, g, gain, send, got, u, e32, dv)
    return out, grad, part


def many_sections(meta, vidx, oidx, vp, op, x, g, gain):
    sections = lax.axis_size("section")
    here = meta[0]
    tokens, width = x.shape
    slots, blk, _ = vp.shape
    wv, we = pl.pallas_call(
        build_dense,
        out_shape=(jax.ShapeDtypeStruct((width, KVW), BF), jax.ShapeDtypeStruct((KVW, width), BF)),
        in_specs=[SMEM] * 3 + [VMEM] * 2,
        out_specs=(VMEM,) * 2,
        scratch_shapes=[pltpu.VMEM((KVW, width), F32)],
        compiler_params=params(),
        name="build_dense",
    )(meta, vidx, oidx, vp, op)
    gain_row = gain.astype(F32)

    def scale(a):
        return lax.rsqrt(jnp.mean(a * a, axis=-1, keepdims=True) + EPS)

    def layer(cur):
        a = cur.astype(F32)
        u = (a * scale(a) * gain_row).astype(BF)
        v = dot(u, wv, NN).astype(BF)
        return (a + dot(v, we, NN)).astype(BF), u

    def fwd(t, cur):
        got = lax.ppermute(layer(cur)[0], "section", [(i, i + 1) for i in range(sections - 1)])
        return jnp.where(here == t + 1, got, cur)

    cur = lax.fori_loop(0, sections - 1, fwd, x)
    out, u = layer(cur)
    a = cur.astype(F32)
    r = scale(a)

    def back(gin):
        dv = dot(gin, we, NT).astype(BF)
        e = dot(dv, wv, NT) * gain_row
        m = jnp.mean(e * a, axis=-1, keepdims=True)
        return (gin.astype(F32) + r * e - r * r * r * a * m).astype(BF), dv

    def bwd(t, gin):
        got = lax.ppermute(back(gin)[0], "section", [(i + 1, i) for i in range(sections - 1)])
        return jnp.where(here == sections - 2 - t, got, gin)

    gin = lax.fori_loop(0, sections - 1, bwd, g)
    grad, dv = back(gin)
    heads = KVW // blk
    picked_in = jnp.take(u.reshape(tokens, -1, blk), vidx[0] // heads, axis=1)
    picked_out = jnp.take(dv.reshape(tokens, heads, blk), vidx[0] % heads, axis=1)
    part = jnp.einsum("tgk,tgn->gkn", picked_in, picked_out, preferred_element_type=F32)
    live = (jnp.arange(slots) < meta[1]).astype(F32) / tokens
    return out, grad, part * live[:, None, None]


def on_device(x, g, gain, value_blocks, output_blocks, vidx, oidx, vcount, ocount):
    sections = lax.axis_size("section")
    here = lax.axis_index("section").astype(jnp.int32)
    vp, op = gather_blocks(value_blocks[0], output_blocks[0])
    meta = jnp.stack([here, vcount[0], ocount[0]])
    run = two_sections if sections == 2 else many_sections
    out, grad, part = run(meta, vidx, oidx, vp, op, x, g, gain)
    vgrad = scatter_grads(part)
    return out[None], grad[None], vgrad[None]


def solution(mesh):
    return jax.shard_map(
        on_device,
        mesh=mesh,
        in_specs=(
            P("dp", None),
            P("dp", None),
            P("section", None),
            P("section", "dp", None, None),
            P("section", "dp", None, None),
            P("section", None),
            P("section", None),
            P("section"),
            P("section"),
        ),
        out_specs=(
            P("section", "dp", None),
            P("section", "dp", None),
            P("section", "dp", None, None),
        ),
        check_vma=False,
    )
```

```python
import jax
import jax.numpy as jnp
from jax import lax
from jax.experimental import pallas as pl
from jax.experimental.pallas import tpu as pltpu
from jax.sharding import PartitionSpec as P

KVW = 1024
HQW = 4096
EPS = 1e-05
BF = jnp.bfloat16
F32 = jnp.float32
ROWS = 16
NN = (((1,), (0,)), ((), ()))
NT = (((1,), (1,)), ((), ()))
VMEM = pl.BlockSpec(memory_space=pltpu.VMEM)
SMEM = pl.BlockSpec(memory_space=pltpu.SMEM)


def dot(a, b, dims):
    return lax.dot_general(a, b, dims, preferred_element_type=F32)


def tile(i, n):
    return pl.ds(pl.multiple_of(i * n, n), n)


def loop(n, body):
    def step(i, c):
        body(i)
        return c

    lax.fori_loop(0, n, step, 0)


def build_dense(meta, vidx, oidx, vp, op, wv, we, acc):
    blk = vp.shape[-1]
    heads = wv.shape[1] // blk
    rows = we.shape[1] // blk
    group = HQW // KVW

    def zero_v(i):
        wv[tile(i, blk), :] = jnp.zeros((blk, wv.shape[1]), BF)

    loop(wv.shape[0] // blk, zero_v)

    def zero_a(i):
        acc[tile(i, 32), :] = jnp.zeros((32, acc.shape[1]), F32)

    loop(acc.shape[0] // 32, zero_a)

    def put_v(j):
        e = vidx[0, j]
        wv[tile(lax.div(e, heads), blk), tile(lax.rem(e, heads), blk)] = vp[j]

    loop(meta[1], put_v)

    def put_o(j):
        e = oidx[0, j]
        r = tile(lax.div(e, rows * group), blk)
        c = tile(lax.rem(e, rows), blk)
        acc[r, c] += op[j].astype(F32)

    loop(meta[2], put_o)

    def cast(i):
        we[tile(i, 32), :] = acc[tile(i, 32), :].astype(BF)

    loop(acc.shape[0] // 32, cast)


def norm(x_ref, gain, u_ref):
    def body(i):
        s = tile(i, ROWS)
        x = x_ref[s, :].astype(F32)
        r = lax.rsqrt(jnp.mean(x * x, axis=-1, keepdims=True) + EPS)
        u_ref[s, :] = (x * r * gain[...].astype(F32)).astype(BF)

    loop(x_ref.shape[0] // ROWS, body)


def forward_values(u_ref, wv, v_ref):
    def body(i):
        c = tile(i, 256)
        v_ref[:, c] = dot(u_ref[...], wv[:, c], NN).astype(BF)

    loop(wv.shape[1] // 256, body)


def forward_mixed(x_ref, v_ref, we, out_ref):
    def body(i):
        c = tile(i, 512)
        m = dot(v_ref[...], we[:, c], NN)
        out_ref[:, c] = (x_ref[:, c].astype(F32) + m).astype(BF)

    loop(we.shape[1] // 512, body)


def backward_values(g_ref, we, dv_ref):
    def body(i):
        c = tile(i, 256)
        dv_ref[:, c] = dot(g_ref[...], we[c, :], NT).astype(BF)

    loop(we.shape[0] // 256, body)


def backward_gained(dv_ref, wv, gain, e_refs):
    def body(i):
        c = tile(i, 512)
        e = dot(dv_ref[...], wv[c, :], NT) * gain[:, c].astype(F32)
        for ref in e_refs:
            ref[:, c] = e.astype(ref.dtype)

    loop(wv.shape[0] // 512, body)


def backward_norm(g_ref, x_ref, e_ref, out_ref):
    def body(i):
        s = tile(i, ROWS)
        x = x_ref[s, :].astype(F32)
        e = e_ref[s, :].astype(F32)
        r = lax.rsqrt(jnp.mean(x * x, axis=-1, keepdims=True) + EPS)
        m = jnp.mean(e * x, axis=-1, keepdims=True)
        out_ref[s, :] = (g_ref[s, :].astype(F32) + r * e - (r * r * r * m) * x).astype(BF)

    loop(x_ref.shape[0] // ROWS, body)


def flip(u_ref, ut_ref):
    blk = ut_ref.shape[1]

    def body(i):
        ut_ref[i] = u_ref[:, tile(i, blk)].T

    loop(ut_ref.shape[0], body)


def params():
    return pltpu.CompilerParams(vmem_limit_bytes=62 << 20)


def own_plan():
    return lax.axis_size("section") == 2 and lax.axis_size("dp") == 16


class Links:
    def __init__(self):
        me = lax.axis_index("dp")
        self.me = me
        self.z, self.y, self.c = lax.div(me, 4), lax.rem(lax.div(me, 2), 2), lax.rem(me, 2)
        self.up, self.down = me + 4, me - 4
        self.has_up, self.has_down = self.z < 3, self.z > 0
        self.side = me + 2 - 4 * self.y
        self.twin = me + 1 - 2 * self.c

    def greet(self, chain):
        barrier = pltpu.get_barrier_semaphore()

        def hello(dev):
            pl.semaphore_signal(barrier, inc=1, device_id={"dp": dev}, device_id_type=pl.DeviceIdType.MESH)

        hello(self.side)
        hello(self.twin)
        if chain:
            pl.when(self.has_up)(lambda: hello(self.up))
            pl.when(self.has_down)(lambda: hello(self.down))
            pl.semaphore_wait(barrier, 2 + (self.has_up).astype(jnp.int32) + (self.has_down).astype(jnp.int32))
        else:
            for k in range(1, 4):
                hello(lax.rem(self.z + k, 4) * 4 + lax.rem(self.me, 4))
            pl.semaphore_wait(barrier, 6)


def remote(src, dst, send_sem, recv_sem, dev):
    return pltpu.make_async_remote_copy(
        src_ref=src,
        dst_ref=dst,
        send_sem=send_sem,
        recv_sem=recv_sem,
        device_id={"dp": dev},
        device_id_type=pl.DeviceIdType.MESH,
    )


def gather_kernel(v_in, o_in, v_all, o_all, send_sem, recv_sem, own_sem):
    at = Links()
    nv, no = v_in.shape[0], o_in.shape[0]
    half = no // 2
    kinds = ((v_in, v_all, nv, nv, 0), (o_in, o_all, no, half, 0), (o_in, o_all, no, half, half))
    own_v = pltpu.make_async_copy(v_in, v_all.at[pl.ds(at.me * nv, nv)], own_sem.at[0])
    own_o = pltpu.make_async_copy(o_in, o_all.at[pl.ds(at.me * no, no)], own_sem.at[1])
    own_v.start()
    own_o.start()
    at.greet(True)
    started = []

    def place(kind, origin):
        _, ref, stride, size, base = kinds[kind]
        return ref.at[pl.ds(origin * stride + base, size)]

    def send(kind, origin, own, way, dev, when):
        ref, _, _, size, base = kinds[kind]
        src = ref.at[pl.ds(base, size)] if own else place(kind, origin)
        lane = lax.div(origin, 2)
        copy = remote(src, place(kind, origin), send_sem.at[kind, lane, way], recv_sem.at[kind, origin], dev)
        if when is None:
            copy.start()
        else:
            pl.when(when)(copy.start)
        return copy, when

    def wait(kind, origin):
        dst = place(kind, origin)
        remote(dst, dst, send_sem.at[kind, 0, 0], recv_sem.at[kind, origin], at.twin).wait_recv()

    def finish(copy, when):
        if when is None:
            copy.wait_send()
        else:
            pl.when(when)(copy.wait_send)

    for kind in (1, 0, 2):
        started.append(send(kind, at.me, True, 0, at.up, at.has_up))
        started.append(send(kind, at.me, True, 1, at.down, at.has_down))
        started.append(send(kind, at.me, True, 2, at.side, None))
        started.append(send(kind, at.me, True, 3, at.twin, None))
    wait(0, at.side)
    started.append(send(0, at.side, False, 0, at.up, at.has_up))
    started.append(send(0, at.side, False, 1, at.down, at.has_down))
    started.append(send(0, at.side, False, 3, at.twin, None))
    tails = []

    for hop in (1, 2, 3):
        for kind, swap in ((1, False), (0, False), (2, False), (0, True)):
            for sign in (-1, 1):
                far = at.z + sign * hop
                there = (far >= 0) & (far < 4)
                origin = (at.side if swap else at.me) + 4 * sign * hop

                def relay(kind=kind, origin=origin, sign=sign):
                    wait(kind, origin)
                    if sign < 0:
                        send(kind, origin, False, 0, at.up, at.has_up)
                    else:
                        send(kind, origin, False, 1, at.down, at.has_down)
                    if kind > 0:
                        send(kind, origin, False, 2, at.side, None)
                    send(kind, origin, False, 3, at.twin, None)

                def ended(kind=kind, origin=origin, sign=sign):
                    def gone(way, dev):
                        src = place(kind, origin)
                        lane = lax.div(origin, 2)
                        return remote(src, src, send_sem.at[kind, lane, way], recv_sem.at[kind, origin], dev).wait_send

                    if sign < 0:
                        pl.when(at.has_up)(gone(0, at.up))
                    else:
                        pl.when(at.has_down)(gone(1, at.down))
                    if kind > 0:
                        gone(2, at.side)()
                    gone(3, at.twin)()

                pl.when(there)(relay)
                tails.append((there, ended))
        for sign in (-1, 1) if hop > 1 else (0,):
            far = at.z + sign * (hop - 1)
            side_block(at, wait, send, started, tails, far, at.side + 4 * sign * (hop - 1), place, send_sem, recv_sem)
    for sign in (-1, 1):
        side_block(at, wait, send, started, tails, at.z + sign * 3, at.side + 12 * sign, place, send_sem, recv_sem)
    for copy, when in started:
        finish(copy, when)
    for there, ended in tails:
        pl.when(there)(ended)
    for k in range(8):
        for kind in range(3):
            wait(kind, 2 * k + 1 - at.c)
    own_v.wait()
    own_o.wait()


def side_block(at, wait, send, started, tails, far, origin, place, send_sem, recv_sem):
    there = (far >= 0) & (far < 4)

    def relay():
        for kind in (1, 2):
            wait(kind, origin)
            send(kind, origin, False, 3, at.twin, None)

    def ended():
        for kind in (1, 2):
            src = place(kind, origin)
            lane = lax.div(origin, 2)
            remote(src, src, send_sem.at[kind, lane, 3], recv_sem.at[kind, origin], at.twin).wait_send()

    pl.when(there)(relay)
    tails.append((there, ended))


def gather_blocks(value_blocks, output_blocks):
    count = lax.axis_size("dp")
    if not own_plan():
        return tuple(lax.all_gather(b, "dp", axis=0, tiled=True) for b in (value_blocks, output_blocks))
    any_space = pl.BlockSpec(memory_space=pl.ANY)

    def whole(b):
        return jax.ShapeDtypeStruct((b.shape[0] * count,) + b.shape[1:], b.dtype)

    return pl.pallas_call(
        gather_kernel,
        out_shape=(whole(value_blocks), whole(output_blocks)),
        in_specs=[any_space] * 2,
        out_specs=(any_space,) * 2,
        scratch_shapes=[
            pltpu.SemaphoreType.DMA((3, 8, 4)),
            pltpu.SemaphoreType.DMA((3, 16)),
            pltpu.SemaphoreType.DMA((2,)),
        ],
        compiler_params=pltpu.CompilerParams(collective_id=0, has_side_effects=True),
        name="gather_blocks",
    )(value_blocks, output_blocks)


def layers_kernel(rows, heads, live, wv, we, x, g, gain, out, grad, vgrad, *scratch):
    got, ebf, u, ut, e32, g1, dv, dvb, v, part, got1, sum1, send2, got2, send3, got3, swap_sem, send_sem, recv_sem = scratch
    at = Links()
    section = lax.axis_index("section")
    barrier = pltpu.get_barrier_semaphore()
    pl.semaphore_signal(
        barrier, inc=1, device_id={"section": 1 - section}, device_id_type=pl.DeviceIdType.MESH
    )
    at.greet(False)
    width = x.shape[1]
    chips, cores, n, blk, _ = part.shape
    chunk = 512
    chunks = width // chunk

    def swap(src, i):
        cols = tile(i, chunk)
        return pltpu.make_async_remote_copy(
            src_ref=src.at[:, cols],
            dst_ref=got.at[:, cols],
            send_sem=swap_sem.at[0, i],
            recv_sem=swap_sem.at[1, i],
            device_id={"section": 1 - section},
            device_id_type=pl.DeviceIdType.MESH,
        )

    @pl.when(section == 0)
    def _():
        norm(x, gain, u)
        forward_values(u, wv, v)

        def mixed(i):
            cols = tile(i, chunk)
            m = dot(v[...], we[:, cols], NN)
            out[:, cols] = (x[:, cols].astype(F32) + m).astype(BF)
            swap(out, i).start()

        loop(chunks, mixed)
        flip(u, ut)

    @pl.when(section == 1)
    def _():
        backward_values(g, we, dv)

        def gained(i):
            cols = tile(i, chunk)
            e = dot(dv[...], wv[cols, :], NT) * gain[:, cols].astype(F32)
            e32[:, cols] = e
            ebf[:, cols] = e.astype(BF)
            swap(ebf, i).start()

        loop(chunks, gained)

    loop(chunks, lambda i: swap(ebf, i).wait_recv())

    @pl.when(section == 0)
    def _():
        backward_norm(g, out, got, g1)
        backward_values(g1, we, dv)

    @pl.when(section == 1)
    def _():
        norm(got, gain, u)
        flip(u, ut)

    def by_head(h):
        dvb[h] = dv[:, tile(h, blk)]

    loop(dvb.shape[0], by_head)

    def slots(k, core):
        for i in range(n):
            j = (k * 2 + core) * n + i
            part[k, core, i] = dot(ut[rows[j]], dvb[heads[j]], NN) * live[j]

    def to_twin(k):
        return remote(part.at[k, 1 - at.c], got1.at[k], send_sem.at[k], recv_sem.at[k], at.twin)

    def for_twin(k):
        slots(k, 1 - at.c)
        to_twin(k).start()

    loop(chips, for_twin)
    loop(chips, lambda k: slots(k, at.c))
    second = []
    for z in range(4):
        for k in (2 * z, 2 * z + 1):
            to_twin(k).wait_recv()
            sum1[k] = part[k, at.c] + got1[k]
        send2[z] = sum1[2 * z + 1 - at.y].astype(BF)
        copy = remote(send2.at[z], got2.at[z], send_sem.at[8 + z], recv_sem.at[8 + z], at.side)
        copy.start()
        second.append(copy)

    @pl.when(section == 0)
    def _():
        backward_gained(dv, wv, gain, (e32,))

    @pl.when(section == 1)
    def _():
        backward_norm(g, got, e32, grad)
        forward_values(u, wv, v)

    for z in range(4):
        second[z].wait_recv()
        k = 2 * z + at.y
        total = sum1[k] + got2[z].astype(F32)
        sum1[k] = total
        send3[z] = total.astype(BF)

        @pl.when(at.z != z)
        def _():
            remote(
                send3.at[z], got3.at[at.z], send_sem.at[12 + z], recv_sem.at[12 + at.z], z * 4 + lax.rem(at.me, 4)
            ).start()

    @pl.when(section == 0)
    def _():
        backward_norm(g1, x, e32, grad)

    @pl.when(section == 1)
    def _():
        forward_mixed(got, v, we, out)

    vgrad[...] = sum1[2 * at.z + at.y]
    for z in range(4):

        @pl.when(at.z != z)
        def _():
            copy = remote(
                send3.at[z], got3.at[z], send_sem.at[12 + z], recv_sem.at[12 + z], z * 4 + lax.rem(at.me, 4)
            )
            copy.wait_recv()
            copy.wait_send()
            vgrad[...] += got3[z].astype(F32)

    for copy in second:
        copy.wait_send()
    loop(chips, lambda k: to_twin(k).wait_send())
    loop(chunks, lambda i: swap(ebf, i).wait_send())


def two_sections(meta, vidx, oidx, vp, op, x, g, gain):
    tokens, width = x.shape
    slots, blk, _ = vp.shape
    n = slots // lax.axis_size("dp")
    wide = jax.ShapeDtypeStruct((tokens, width), BF)
    heads = KVW // blk
    live = (jnp.arange(slots) < meta[1]).astype(F32) / tokens
    wv, we = dense_weights(meta, vidx, oidx, vp, op, width)
    return pl.pallas_call(
        layers_kernel,
        out_shape=(wide, wide, jax.ShapeDtypeStruct((n, blk, blk), F32)),
        in_specs=[SMEM] * 3 + [VMEM] * 5,
        out_specs=(VMEM,) * 3,
        scratch_shapes=[
            pltpu.VMEM((tokens, width), BF),
            pltpu.VMEM((tokens, width), BF),
            pltpu.VMEM((tokens, width), BF),
            pltpu.VMEM((width // blk, blk, tokens), BF),
            pltpu.VMEM((tokens, width), F32),
            pltpu.VMEM((tokens, width), BF),
            pltpu.VMEM((tokens, KVW), BF),
            pltpu.VMEM((KVW // blk, tokens, blk), BF),
            pltpu.VMEM((tokens, KVW), BF),
            pltpu.VMEM((8, 2, n, blk, blk), F32),
            pltpu.VMEM((8, n, blk, blk), F32),
            pltpu.VMEM((8, n, blk, blk), F32),
            pltpu.VMEM((4, n, blk, blk), BF),
            pltpu.VMEM((4, n, blk, blk), BF),
            pltpu.VMEM((4, n, blk, blk), BF),
            pltpu.VMEM((4, n, blk, blk), BF),
            pltpu.SemaphoreType.DMA((2, width // 512)),
            pltpu.SemaphoreType.DMA((16,)),
            pltpu.SemaphoreType.DMA((16,)),
        ],
        compiler_params=pltpu.CompilerParams(collective_id=1, has_side_effects=True, vmem_limit_bytes=60 << 20),
        name="layers",
    )(vidx[0] // heads, vidx[0] % heads, live, wv, we, x, g, gain)


def dense_weights(meta, vidx, oidx, vp, op, width):
    return pl.pallas_call(
        build_dense,
        out_shape=(jax.ShapeDtypeStruct((width, KVW), BF), jax.ShapeDtypeStruct((KVW, width), BF)),
        in_specs=[SMEM] * 3 + [VMEM] * 2,
        out_specs=(VMEM,) * 2,
        scratch_shapes=[pltpu.VMEM((KVW, width), F32)],
        compiler_params=params(),
        name="build_dense",
    )(meta, vidx, oidx, vp, op)


def many_sections(meta, vidx, oidx, vp, op, x, g, gain):
    sections = lax.axis_size("section")
    here = meta[0]
    tokens, width = x.shape
    slots, blk, _ = vp.shape
    wv, we = dense_weights(meta, vidx, oidx, vp, op, width)
    gain_row = gain.astype(F32)

    def scale(a):
        return lax.rsqrt(jnp.mean(a * a, axis=-1, keepdims=True) + EPS)

    def layer(cur):
        a = cur.astype(F32)
        u = (a * scale(a) * gain_row).astype(BF)
        v = dot(u, wv, NN).astype(BF)
        return (a + dot(v, we, NN)).astype(BF), u

    def fwd(t, cur):
        got = lax.ppermute(layer(cur)[0], "section", [(i, i + 1) for i in range(sections - 1)])
        return jnp.where(here == t + 1, got, cur)

    cur = lax.fori_loop(0, sections - 1, fwd, x)
    out, u = layer(cur)
    a = cur.astype(F32)
    r = scale(a)

    def back(gin):
        dv = dot(gin, we, NT).astype(BF)
        e = dot(dv, wv, NT) * gain_row
        m = jnp.mean(e * a, axis=-1, keepdims=True)
        return (gin.astype(F32) + r * e - r * r * r * a * m).astype(BF), dv

    def bwd(t, gin):
        got = lax.ppermute(back(gin)[0], "section", [(i + 1, i) for i in range(sections - 1)])
        return jnp.where(here == sections - 2 - t, got, gin)

    gin = lax.fori_loop(0, sections - 1, bwd, g)
    grad, dv = back(gin)
    heads = KVW // blk
    picked_in = jnp.take(u.reshape(tokens, -1, blk), vidx[0] // heads, axis=1)
    picked_out = jnp.take(dv.reshape(tokens, heads, blk), vidx[0] % heads, axis=1)
    part = jnp.einsum("tgk,tgn->gkn", picked_in, picked_out, preferred_element_type=F32)
    live = (jnp.arange(slots) < meta[1]).astype(F32) / tokens
    part = part * live[:, None, None]
    return out, grad, lax.psum_scatter(part, "dp", scatter_dimension=0, tiled=True)


def on_device(x, g, gain, value_blocks, output_blocks, vidx, oidx, vcount, ocount):
    here = lax.axis_index("section").astype(jnp.int32)
    vp, op = gather_blocks(value_blocks[0], output_blocks[0])
    meta = jnp.stack([here, vcount[0], ocount[0]])
    run = two_sections if own_plan() else many_sections
    out, grad, vgrad = run(meta, vidx, oidx, vp, op, x, g, gain)
    return out[None], grad[None], vgrad[None]


def solution(mesh):
    return jax.shard_map(
        on_device,
        mesh=mesh,
        in_specs=(
            P("dp", None),
            P("dp", None),
            P("section", None),
            P("section", "dp", None, None),
            P("section", "dp", None, None),
            P("section", None),
            P("section", None),
            P("section"),
            P("section"),
        ),
        out_specs=(
            P("section", "dp", None),
            P("section", "dp", None),
            P("section", "dp", None, None),
        ),
        check_vma=False,
    )
```

```python
import jax
import jax.numpy as jnp
from jax import lax
from jax.experimental import pallas as pl
from jax.experimental.pallas import tpu as pltpu
from jax.sharding import PartitionSpec as P

KVW = 1024
HQW = 4096
EPS = 1e-05
BF = jnp.bfloat16
F32 = jnp.float32
ROWS = 16
NN = (((1,), (0,)), ((), ()))
NT = (((1,), (1,)), ((), ()))
VMEM = pl.BlockSpec(memory_space=pltpu.VMEM)
SMEM = pl.BlockSpec(memory_space=pltpu.SMEM)


def dot(a, b, dims):
    return lax.dot_general(a, b, dims, preferred_element_type=F32)


def tile(i, n):
    return pl.ds(pl.multiple_of(i * n, n), n)


def loop(n, body):
    def step(i, c):
        body(i)
        return c

    lax.fori_loop(0, n, step, 0)


def build_dense(meta, vidx, oidx, vp_in, op_in, wv_out, we_out, vp, op, wv, we, acc, sem):
    load_v = pltpu.make_async_copy(vp_in, vp, sem.at[0])
    load_o = pltpu.make_async_copy(op_in, op, sem.at[1])
    save_v = pltpu.make_async_copy(wv, wv_out, sem.at[2])
    load_v.start()
    load_o.start()
    blk = vp.shape[-1]
    heads = wv.shape[1] // blk
    rows = we.shape[1] // blk
    group = HQW // KVW

    def zero_v(i):
        wv[tile(i, blk), :] = jnp.zeros((blk, wv.shape[1]), BF)

    loop(wv.shape[0] // blk, zero_v)

    def zero_a(i):
        acc[tile(i, 32), :] = jnp.zeros((32, acc.shape[1]), F32)

    loop(acc.shape[0] // 32, zero_a)

    def put_v(j):
        e = vidx[0, j]
        wv[tile(lax.div(e, heads), blk), tile(lax.rem(e, heads), blk)] = vp[j]

    load_v.wait()
    loop(meta[1], put_v)
    save_v.start()

    def put_o(j):
        e = oidx[0, j]
        r = tile(lax.div(e, rows * group), blk)
        c = tile(lax.rem(e, rows), blk)
        acc[r, c] += op[j].astype(F32)

    load_o.wait()
    loop(meta[2], put_o)

    def save(i):
        return pltpu.make_async_copy(we.at[tile(i, blk), :], we_out.at[tile(i, blk), :], sem.at[3 + i])

    def cast(i):
        for k in range(0, blk, 32):
            rows_k = pl.ds(pl.multiple_of(i * blk + k, 32), 32)
            we[rows_k, :] = acc[rows_k, :].astype(BF)
        save(i).start()

    loop(heads, cast)
    save_v.wait()
    loop(heads, lambda i: save(i).wait())


def norm(x_ref, gain, u_ref):
    def body(i):
        s = tile(i, ROWS)
        x = x_ref[s, :].astype(F32)
        r = lax.rsqrt(jnp.mean(x * x, axis=-1, keepdims=True) + EPS)
        u_ref[s, :] = (x * r * gain[...].astype(F32)).astype(BF)

    loop(x_ref.shape[0] // ROWS, body)


def forward_values(u_ref, wv, v_ref):
    def body(i):
        c = tile(i, 256)
        v_ref[:, c] = dot(u_ref[...], wv[:, c], NN).astype(BF)

    loop(wv.shape[1] // 256, body)


def forward_mixed(x_ref, v_ref, we, out_ref):
    def body(i):
        c = tile(i, 512)
        m = dot(v_ref[...], we[:, c], NN)
        out_ref[:, c] = (x_ref[:, c].astype(F32) + m).astype(BF)

    loop(we.shape[1] // 512, body)


def backward_values(g_ref, we, dv_ref):
    def body(i):
        c = tile(i, 256)
        dv_ref[:, c] = dot(g_ref[...], we[c, :], NT).astype(BF)

    loop(we.shape[0] // 256, body)


def backward_gained(dv_ref, wv, gain, e_refs):
    def body(i):
        c = tile(i, 512)
        e = dot(dv_ref[...], wv[c, :], NT) * gain[:, c].astype(F32)
        for ref in e_refs:
            ref[:, c] = e.astype(ref.dtype)

    loop(wv.shape[0] // 512, body)


def backward_norm(g_ref, x_ref, e_ref, out_ref):
    def body(i):
        s = tile(i, ROWS)
        x = x_ref[s, :].astype(F32)
        e = e_ref[s, :].astype(F32)
        r = lax.rsqrt(jnp.mean(x * x, axis=-1, keepdims=True) + EPS)
        m = jnp.mean(e * x, axis=-1, keepdims=True)
        out_ref[s, :] = (g_ref[s, :].astype(F32) + r * e - (r * r * r * m) * x).astype(BF)

    loop(x_ref.shape[0] // ROWS, body)


def flip(u_ref, ut_ref):
    blk = ut_ref.shape[1]

    def body(i):
        ut_ref[i] = u_ref[:, tile(i, blk)].T

    loop(ut_ref.shape[0], body)


def params():
    return pltpu.CompilerParams(vmem_limit_bytes=62 << 20)


def own_plan():
    return lax.axis_size("section") == 2 and lax.axis_size("dp") == 16


class Links:
    def __init__(self):
        me = lax.axis_index("dp")
        self.me = me
        self.z, self.y, self.c = lax.div(me, 4), lax.rem(lax.div(me, 2), 2), lax.rem(me, 2)
        self.up, self.down = me + 4, me - 4
        self.has_up, self.has_down = self.z < 3, self.z > 0
        self.side = me + 2 - 4 * self.y
        self.twin = me + 1 - 2 * self.c

    def greet(self, chain):
        barrier = pltpu.get_barrier_semaphore()

        def hello(dev):
            pl.semaphore_signal(barrier, inc=1, device_id={"dp": dev}, device_id_type=pl.DeviceIdType.MESH)

        hello(self.side)
        hello(self.twin)
        if chain:
            pl.when(self.has_up)(lambda: hello(self.up))
            pl.when(self.has_down)(lambda: hello(self.down))
            pl.semaphore_wait(barrier, 2 + (self.has_up).astype(jnp.int32) + (self.has_down).astype(jnp.int32))
        else:
            for k in range(1, 4):
                hello(lax.rem(self.z + k, 4) * 4 + lax.rem(self.me, 4))
            pl.semaphore_wait(barrier, 6)


def remote(src, dst, send_sem, recv_sem, dev):
    return pltpu.make_async_remote_copy(
        src_ref=src,
        dst_ref=dst,
        send_sem=send_sem,
        recv_sem=recv_sem,
        device_id={"dp": dev},
        device_id_type=pl.DeviceIdType.MESH,
    )


def gather_kernel(v_in, o_in, v_all, o_all, send_sem, recv_sem, own_sem):
    at = Links()
    nv, no = v_in.shape[0], o_in.shape[0]
    part = no // 4
    kinds = ((v_in, v_all, nv, nv, 0),) + tuple((o_in, o_all, no, part, i * part) for i in range(4))
    own_v = pltpu.make_async_copy(v_in, v_all.at[pl.ds(at.me * nv, nv)], own_sem.at[0])
    own_o = pltpu.make_async_copy(o_in, o_all.at[pl.ds(at.me * no, no)], own_sem.at[1])
    own_v.start()
    own_o.start()
    at.greet(True)
    started = []

    def place(kind, origin):
        _, ref, stride, size, base = kinds[kind]
        return ref.at[pl.ds(origin * stride + base, size)]

    def send(kind, origin, own, way, dev, when):
        ref, _, _, size, base = kinds[kind]
        src = ref.at[pl.ds(base, size)] if own else place(kind, origin)
        lane = lax.div(origin, 2)
        copy = remote(src, place(kind, origin), send_sem.at[kind, lane, way], recv_sem.at[kind, origin], dev)
        if when is None:
            copy.start()
        else:
            pl.when(when)(copy.start)
        return copy, when

    def wait(kind, origin):
        dst = place(kind, origin)
        remote(dst, dst, send_sem.at[kind, 0, 0], recv_sem.at[kind, origin], at.twin).wait_recv()

    def finish(copy, when):
        if when is None:
            copy.wait_send()
        else:
            pl.when(when)(copy.wait_send)

    for kind in (1, 0, 2, 3, 4):
        started.append(send(kind, at.me, True, 0, at.up, at.has_up))
        started.append(send(kind, at.me, True, 1, at.down, at.has_down))
        started.append(send(kind, at.me, True, 2, at.side, None))
        started.append(send(kind, at.me, True, 3, at.twin, None))
    wait(0, at.side)
    started.append(send(0, at.side, False, 0, at.up, at.has_up))
    started.append(send(0, at.side, False, 1, at.down, at.has_down))
    started.append(send(0, at.side, False, 3, at.twin, None))
    tails = []

    for hop in (1, 2, 3):
        for kind, swap in ((1, False), (2, False), (0, False), (3, False), (4, False), (0, True)):
            for sign in (-1, 1):
                far = at.z + sign * hop
                there = (far >= 0) & (far < 4)
                origin = (at.side if swap else at.me) + 4 * sign * hop

                def relay(kind=kind, origin=origin, sign=sign):
                    wait(kind, origin)
                    if sign < 0:
                        send(kind, origin, False, 0, at.up, at.has_up)
                    else:
                        send(kind, origin, False, 1, at.down, at.has_down)
                    if kind > 0:
                        send(kind, origin, False, 2, at.side, None)
                    send(kind, origin, False, 3, at.twin, None)

                def ended(kind=kind, origin=origin, sign=sign):
                    def gone(way, dev):
                        src = place(kind, origin)
                        lane = lax.div(origin, 2)
                        return remote(src, src, send_sem.at[kind, lane, way], recv_sem.at[kind, origin], dev).wait_send

                    if sign < 0:
                        pl.when(at.has_up)(gone(0, at.up))
                    else:
                        pl.when(at.has_down)(gone(1, at.down))
                    if kind > 0:
                        gone(2, at.side)()
                    gone(3, at.twin)()

                pl.when(there)(relay)
                tails.append((there, ended))
        for sign in (-1, 1) if hop > 1 else (0,):
            far = at.z + sign * (hop - 1)
            side_block(at, wait, send, started, tails, far, at.side + 4 * sign * (hop - 1), place, send_sem, recv_sem)
    for sign in (-1, 1):
        side_block(at, wait, send, started, tails, at.z + sign * 3, at.side + 12 * sign, place, send_sem, recv_sem)
    for copy, when in started:
        finish(copy, when)
    for there, ended in tails:
        pl.when(there)(ended)
    for k in range(8):
        for kind in range(5):
            wait(kind, 2 * k + 1 - at.c)
    own_v.wait()
    own_o.wait()


def side_block(at, wait, send, started, tails, far, origin, place, send_sem, recv_sem):
    there = (far >= 0) & (far < 4)

    def relay():
        for kind in (1, 2, 3, 4):
            wait(kind, origin)
            send(kind, origin, False, 3, at.twin, None)

    def ended():
        for kind in (1, 2, 3, 4):
            src = place(kind, origin)
            lane = lax.div(origin, 2)
            remote(src, src, send_sem.at[kind, lane, 3], recv_sem.at[kind, origin], at.twin).wait_send()

    pl.when(there)(relay)
    tails.append((there, ended))


def gather_blocks(value_blocks, output_blocks):
    count = lax.axis_size("dp")
    if not own_plan():
        return tuple(lax.all_gather(b, "dp", axis=0, tiled=True) for b in (value_blocks, output_blocks))
    any_space = pl.BlockSpec(memory_space=pl.ANY)

    def whole(b):
        return jax.ShapeDtypeStruct((b.shape[0] * count,) + b.shape[1:], b.dtype)

    return pl.pallas_call(
        gather_kernel,
        out_shape=(whole(value_blocks), whole(output_blocks)),
        in_specs=[any_space] * 2,
        out_specs=(any_space,) * 2,
        scratch_shapes=[
            pltpu.SemaphoreType.DMA((5, 8, 4)),
            pltpu.SemaphoreType.DMA((5, 16)),
            pltpu.SemaphoreType.DMA((2,)),
        ],
        compiler_params=pltpu.CompilerParams(collective_id=0, has_side_effects=True),
        name="gather_blocks",
    )(value_blocks, output_blocks)


def layers_kernel(rows, heads, live, wv_in, we_in, x, g, gain, out, grad, vgrad, *scratch):
    got, ebf, u, ut, e32, g1, dv, dvb, v, part, got1, sum1, send2, got2, send3, got3, swap_sem, send_sem, recv_sem, wv, we, load_sem = scratch
    load_v = pltpu.make_async_copy(wv_in, wv, load_sem.at[0])
    load_o = pltpu.make_async_copy(we_in, we, load_sem.at[1])
    load_v.start()
    load_o.start()
    at = Links()
    section = lax.axis_index("section")
    barrier = pltpu.get_barrier_semaphore()
    pl.semaphore_signal(
        barrier, inc=1, device_id={"section": 1 - section}, device_id_type=pl.DeviceIdType.MESH
    )
    at.greet(False)
    width = x.shape[1]
    chips, cores, n, blk, _ = part.shape
    chunk = 512
    chunks = width // chunk

    def swap(src, i):
        cols = tile(i, chunk)
        return pltpu.make_async_remote_copy(
            src_ref=src.at[:, cols],
            dst_ref=got.at[:, cols],
            send_sem=swap_sem.at[0, i],
            recv_sem=swap_sem.at[1, i],
            device_id={"section": 1 - section},
            device_id_type=pl.DeviceIdType.MESH,
        )

    @pl.when(section == 0)
    def _():
        norm(x, gain, u)
        load_v.wait()
        forward_values(u, wv, v)
        load_o.wait()

        def mixed(i):
            cols = tile(i, chunk)
            m = dot(v[...], we[:, cols], NN)
            out[:, cols] = (x[:, cols].astype(F32) + m).astype(BF)
            swap(out, i).start()

        loop(chunks, mixed)
        flip(u, ut)

    @pl.when(section == 1)
    def _():
        load_o.wait()
        backward_values(g, we, dv)
        load_v.wait()

        def gained(i):
            cols = tile(i, chunk)
            e = dot(dv[...], wv[cols, :], NT) * gain[:, cols].astype(F32)
            e32[:, cols] = e
            ebf[:, cols] = e.astype(BF)
            swap(ebf, i).start()

        loop(chunks, gained)

    loop(chunks, lambda i: swap(ebf, i).wait_recv())

    @pl.when(section == 0)
    def _():
        backward_norm(g, out, got, g1)
        backward_values(g1, we, dv)

    @pl.when(section == 1)
    def _():
        norm(got, gain, u)
        flip(u, ut)

    def by_head(h):
        dvb[h] = dv[:, tile(h, blk)]

    loop(dvb.shape[0], by_head)

    def slots(k, core):
        for i in range(n):
            j = (k * 2 + core) * n + i
            part[k, core, i] = dot(ut[rows[j]], dvb[heads[j]], NN) * live[j]

    def to_twin(k):
        return remote(part.at[k, 1 - at.c], got1.at[k], send_sem.at[k], recv_sem.at[k], at.twin)

    def for_twin(k):
        slots(k, 1 - at.c)
        to_twin(k).start()

    loop(chips, for_twin)
    loop(chips, lambda k: slots(k, at.c))
    second = []
    for z in range(4):
        for k in (2 * z, 2 * z + 1):
            to_twin(k).wait_recv()
            sum1[k] = part[k, at.c] + got1[k]
        send2[z] = sum1[2 * z + 1 - at.y].astype(BF)
        copy = remote(send2.at[z], got2.at[z], send_sem.at[8 + z], recv_sem.at[8 + z], at.side)
        copy.start()
        second.append(copy)

    @pl.when(section == 0)
    def _():
        backward_gained(dv, wv, gain, (e32,))

    @pl.when(section == 1)
    def _():
        backward_norm(g, got, e32, grad)
        forward_values(u, wv, v)

    for z in range(4):
        second[z].wait_recv()
        k = 2 * z + at.y
        total = sum1[k] + got2[z].astype(F32)
        sum1[k] = total
        send3[z] = total.astype(BF)

        @pl.when(at.z != z)
        def _():
            remote(
                send3.at[z], got3.at[at.z], send_sem.at[12 + z], recv_sem.at[12 + at.z], z * 4 + lax.rem(at.me, 4)
            ).start()

    @pl.when(section == 0)
    def _():
        backward_norm(g1, x, e32, grad)

    @pl.when(section == 1)
    def _():
        forward_mixed(got, v, we, out)

    vgrad[...] = sum1[2 * at.z + at.y]
    for z in range(4):

        @pl.when(at.z != z)
        def _():
            copy = remote(
                send3.at[z], got3.at[z], send_sem.at[12 + z], recv_sem.at[12 + z], z * 4 + lax.rem(at.me, 4)
            )
            copy.wait_recv()
            copy.wait_send()
            vgrad[...] += got3[z].astype(F32)

    for copy in second:
        copy.wait_send()
    loop(chips, lambda k: to_twin(k).wait_send())
    loop(chunks, lambda i: swap(ebf, i).wait_send())


def two_sections(meta, vidx, oidx, vp, op, x, g, gain):
    tokens, width = x.shape
    slots, blk, _ = vp.shape
    n = slots // lax.axis_size("dp")
    wide = jax.ShapeDtypeStruct((tokens, width), BF)
    heads = KVW // blk
    live = (jnp.arange(slots) < meta[1]).astype(F32) / tokens
    wv, we = dense_weights(meta, vidx, oidx, vp, op, width)
    return pl.pallas_call(
        layers_kernel,
        out_shape=(wide, wide, jax.ShapeDtypeStruct((n, blk, blk), F32)),
        in_specs=[SMEM] * 3 + [pl.BlockSpec(memory_space=pl.ANY)] * 2 + [VMEM] * 3,
        out_specs=(VMEM,) * 3,
        scratch_shapes=[
            pltpu.VMEM((tokens, width), BF),
            pltpu.VMEM((tokens, width), BF),
            pltpu.VMEM((tokens, width), BF),
            pltpu.VMEM((width // blk, blk, tokens), BF),
            pltpu.VMEM((tokens, width), F32),
            pltpu.VMEM((tokens, width), BF),
            pltpu.VMEM((tokens, KVW), BF),
            pltpu.VMEM((KVW // blk, tokens, blk), BF),
            pltpu.VMEM((tokens, KVW), BF),
            pltpu.VMEM((8, 2, n, blk, blk), F32),
            pltpu.VMEM((8, n, blk, blk), F32),
            pltpu.VMEM((8, n, blk, blk), F32),
            pltpu.VMEM((4, n, blk, blk), BF),
            pltpu.VMEM((4, n, blk, blk), BF),
            pltpu.VMEM((4, n, blk, blk), BF),
            pltpu.VMEM((4, n, blk, blk), BF),
            pltpu.SemaphoreType.DMA((2, width // 512)),
            pltpu.SemaphoreType.DMA((16,)),
            pltpu.SemaphoreType.DMA((16,)),
            pltpu.VMEM((width, KVW), BF),
            pltpu.VMEM((KVW, width), BF),
            pltpu.SemaphoreType.DMA((2,)),
        ],
        compiler_params=pltpu.CompilerParams(collective_id=1, has_side_effects=True, vmem_limit_bytes=60 << 20),
        name="layers",
    )(vidx[0] // heads, vidx[0] % heads, live, wv, we, x, g, gain)


def dense_weights(meta, vidx, oidx, vp, op, width):
    return pl.pallas_call(
        build_dense,
        out_shape=(jax.ShapeDtypeStruct((width, KVW), BF), jax.ShapeDtypeStruct((KVW, width), BF)),
        in_specs=[SMEM] * 3 + [pl.BlockSpec(memory_space=pl.ANY)] * 2,
        out_specs=(pl.BlockSpec(memory_space=pl.ANY),) * 2,
        scratch_shapes=[
            pltpu.VMEM(vp.shape, BF),
            pltpu.VMEM(op.shape, BF),
            pltpu.VMEM((width, KVW), BF),
            pltpu.VMEM((KVW, width), BF),
            pltpu.VMEM((KVW, width), F32),
            pltpu.SemaphoreType.DMA((3 + KVW // vp.shape[-1],)),
        ],
        compiler_params=params(),
        name="build_dense",
    )(meta, vidx, oidx, vp, op)


def many_sections(meta, vidx, oidx, vp, op, x, g, gain):
    sections = lax.axis_size("section")
    here = meta[0]
    tokens, width = x.shape
    slots, blk, _ = vp.shape
    wv, we = dense_weights(meta, vidx, oidx, vp, op, width)
    gain_row = gain.astype(F32)

    def scale(a):
        return lax.rsqrt(jnp.mean(a * a, axis=-1, keepdims=True) + EPS)

    def layer(cur):
        a = cur.astype(F32)
        u = (a * scale(a) * gain_row).astype(BF)
        v = dot(u, wv, NN).astype(BF)
        return (a + dot(v, we, NN)).astype(BF), u

    def fwd(t, cur):
        got = lax.ppermute(layer(cur)[0], "section", [(i, i + 1) for i in range(sections - 1)])
        return jnp.where(here == t + 1, got, cur)

    cur = lax.fori_loop(0, sections - 1, fwd, x)
    out, u = layer(cur)
    a = cur.astype(F32)
    r = scale(a)

    def back(gin):
        dv = dot(gin, we, NT).astype(BF)
        e = dot(dv, wv, NT) * gain_row
        m = jnp.mean(e * a, axis=-1, keepdims=True)
        return (gin.astype(F32) + r * e - r * r * r * a * m).astype(BF), dv

    def bwd(t, gin):
        got = lax.ppermute(back(gin)[0], "section", [(i + 1, i) for i in range(sections - 1)])
        return jnp.where(here == sections - 2 - t, got, gin)

    gin = lax.fori_loop(0, sections - 1, bwd, g)
    grad, dv = back(gin)
    heads = KVW // blk
    picked_in = jnp.take(u.reshape(tokens, -1, blk), vidx[0] // heads, axis=1)
    picked_out = jnp.take(dv.reshape(tokens, heads, blk), vidx[0] % heads, axis=1)
    part = jnp.einsum("tgk,tgn->gkn", picked_in, picked_out, preferred_element_type=F32)
    live = (jnp.arange(slots) < meta[1]).astype(F32) / tokens
    part = part * live[:, None, None]
    return out, grad, lax.psum_scatter(part, "dp", scatter_dimension=0, tiled=True)


def on_device(x, g, gain, value_blocks, output_blocks, vidx, oidx, vcount, ocount):
    here = lax.axis_index("section").astype(jnp.int32)
    vp, op = gather_blocks(value_blocks[0], output_blocks[0])
    meta = jnp.stack([here, vcount[0], ocount[0]])
    run = two_sections if own_plan() else many_sections
    out, grad, vgrad = run(meta, vidx, oidx, vp, op, x, g, gain)
    return out[None], grad[None], vgrad[None]


def solution(mesh):
    return jax.shard_map(
        on_device,
        mesh=mesh,
        in_specs=(
            P("dp", None),
            P("dp", None),
            P("section", None),
            P("section", "dp", None, None),
            P("section", "dp", None, None),
            P("section", None),
            P("section", None),
            P("section"),
            P("section"),
        ),
        out_specs=(
            P("section", "dp", None),
            P("section", "dp", None),
            P("section", "dp", None, None),
        ),
        check_vma=False,
    )
```

```python
import jax
import jax.numpy as jnp
from jax import lax
from jax.experimental import pallas as pl
from jax.experimental.pallas import tpu as pltpu
from jax.sharding import PartitionSpec as P

KVW = 1024
HQW = 4096
EPS = 1e-05
BF = jnp.bfloat16
F32 = jnp.float32
ROWS = 16
NN = (((1,), (0,)), ((), ()))
NT = (((1,), (1,)), ((), ()))
VMEM = pl.BlockSpec(memory_space=pltpu.VMEM)
SMEM = pl.BlockSpec(memory_space=pltpu.SMEM)


def dot(a, b, dims):
    return lax.dot_general(a, b, dims, preferred_element_type=F32)


def tile(i, n):
    return pl.ds(pl.multiple_of(i * n, n), n)


def loop(n, body):
    def step(i, c):
        body(i)
        return c

    lax.fori_loop(0, n, step, 0)


def build_dense(meta, vidx, oidx, vp_in, op_in, wv_out, we_out, vp, op, wv, we, acc, sem):
    load_v = pltpu.make_async_copy(vp_in, vp, sem.at[0])
    load_o = pltpu.make_async_copy(op_in, op, sem.at[1])
    save_v = pltpu.make_async_copy(wv, wv_out, sem.at[2])
    load_v.start()
    load_o.start()
    blk = vp.shape[-1]
    heads = wv.shape[1] // blk
    rows = we.shape[1] // blk
    group = HQW // KVW

    def zero_v(i):
        wv[tile(i, blk), :] = jnp.zeros((blk, wv.shape[1]), BF)

    loop(wv.shape[0] // blk, zero_v)

    def zero_a(i):
        acc[tile(i, 32), :] = jnp.zeros((32, acc.shape[1]), F32)

    loop(acc.shape[0] // 32, zero_a)

    def put_v(j):
        e = vidx[0, j]
        wv[tile(lax.div(e, heads), blk), tile(lax.rem(e, heads), blk)] = vp[j]

    load_v.wait()
    loop(meta[1], put_v)
    save_v.start()

    def put_o(j):
        e = oidx[0, j]
        r = tile(lax.div(e, rows * group), blk)
        c = tile(lax.rem(e, rows), blk)
        acc[r, c] += op[j].astype(F32)

    load_o.wait()
    loop(meta[2], put_o)

    def save(i):
        return pltpu.make_async_copy(we.at[tile(i, blk), :], we_out.at[tile(i, blk), :], sem.at[3 + i])

    def cast(i):
        for k in range(0, blk, 32):
            rows_k = pl.ds(pl.multiple_of(i * blk + k, 32), 32)
            we[rows_k, :] = acc[rows_k, :].astype(BF)
        save(i).start()

    loop(heads, cast)
    save_v.wait()
    loop(heads, lambda i: save(i).wait())


def norm(x_ref, gain, u_ref):
    def body(i):
        s = tile(i, ROWS)
        x = x_ref[s, :].astype(F32)
        r = lax.rsqrt(jnp.mean(x * x, axis=-1, keepdims=True) + EPS)
        u_ref[s, :] = (x * r * gain[...].astype(F32)).astype(BF)

    loop(x_ref.shape[0] // ROWS, body)


def forward_values(u_ref, wv, v_ref):
    def body(i):
        c = tile(i, 256)
        v_ref[:, c] = dot(u_ref[...], wv[:, c], NN).astype(BF)

    loop(wv.shape[1] // 256, body)


def forward_mixed(x_ref, v_ref, we, out_ref):
    def body(i):
        c = tile(i, 512)
        m = dot(v_ref[...], we[:, c], NN)
        out_ref[:, c] = (x_ref[:, c].astype(F32) + m).astype(BF)

    loop(we.shape[1] // 512, body)


def backward_values(g_ref, we, dv_ref):
    def body(i):
        c = tile(i, 256)
        dv_ref[:, c] = dot(g_ref[...], we[c, :], NT).astype(BF)

    loop(we.shape[0] // 256, body)


def backward_gained(dv_ref, wv, gain, e_refs):
    def body(i):
        c = tile(i, 512)
        e = dot(dv_ref[...], wv[c, :], NT) * gain[:, c].astype(F32)
        for ref in e_refs:
            ref[:, c] = e.astype(ref.dtype)

    loop(wv.shape[0] // 512, body)


def backward_norm(g_ref, x_ref, e_ref, out_ref):
    def body(i):
        s = tile(i, ROWS)
        x = x_ref[s, :].astype(F32)
        e = e_ref[s, :].astype(F32)
        r = lax.rsqrt(jnp.mean(x * x, axis=-1, keepdims=True) + EPS)
        m = jnp.mean(e * x, axis=-1, keepdims=True)
        out_ref[s, :] = (g_ref[s, :].astype(F32) + r * e - (r * r * r * m) * x).astype(BF)

    loop(x_ref.shape[0] // ROWS, body)


def flip(u_ref, ut_ref):
    blk = ut_ref.shape[1]

    def body(i):
        ut_ref[i] = u_ref[:, tile(i, blk)].T

    loop(ut_ref.shape[0], body)


def params():
    return pltpu.CompilerParams(vmem_limit_bytes=62 << 20)


def own_plan():
    return lax.axis_size("section") == 2 and lax.axis_size("dp") == 16


class Links:
    def __init__(self):
        me = lax.axis_index("dp")
        self.me = me
        self.z, self.y, self.c = lax.div(me, 4), lax.rem(lax.div(me, 2), 2), lax.rem(me, 2)
        self.up, self.down = me + 4, me - 4
        self.has_up, self.has_down = self.z < 3, self.z > 0
        self.side = me + 2 - 4 * self.y
        self.twin = me + 1 - 2 * self.c

    def greet(self, chain):
        barrier = pltpu.get_barrier_semaphore()

        def hello(dev):
            pl.semaphore_signal(barrier, inc=1, device_id={"dp": dev}, device_id_type=pl.DeviceIdType.MESH)

        hello(self.side)
        hello(self.twin)
        if chain:
            pl.when(self.has_up)(lambda: hello(self.up))
            pl.when(self.has_down)(lambda: hello(self.down))
            pl.semaphore_wait(barrier, 2 + (self.has_up).astype(jnp.int32) + (self.has_down).astype(jnp.int32))
        else:
            for k in range(1, 4):
                hello(lax.rem(self.z + k, 4) * 4 + lax.rem(self.me, 4))
            pl.semaphore_wait(barrier, 6)


def remote(src, dst, send_sem, recv_sem, dev):
    return pltpu.make_async_remote_copy(
        src_ref=src,
        dst_ref=dst,
        send_sem=send_sem,
        recv_sem=recv_sem,
        device_id={"dp": dev},
        device_id_type=pl.DeviceIdType.MESH,
    )


def gather_kernel(v_in, o_in, v_all, o_all, send_sem, recv_sem, own_sem):
    at = Links()
    nv, no = v_in.shape[0], o_in.shape[0]
    part = no // 4
    kinds = ((v_in, v_all, nv, nv, 0),) + tuple((o_in, o_all, no, part, i * part) for i in range(4))
    own_v = pltpu.make_async_copy(v_in, v_all.at[pl.ds(at.me * nv, nv)], own_sem.at[0])
    own_o = pltpu.make_async_copy(o_in, o_all.at[pl.ds(at.me * no, no)], own_sem.at[1])
    own_v.start()
    own_o.start()
    at.greet(True)
    started = []

    def place(kind, origin):
        _, ref, stride, size, base = kinds[kind]
        return ref.at[pl.ds(origin * stride + base, size)]

    def send(kind, origin, own, way, dev, when):
        ref, _, _, size, base = kinds[kind]
        src = ref.at[pl.ds(base, size)] if own else place(kind, origin)
        lane = lax.div(origin, 2)
        copy = remote(src, place(kind, origin), send_sem.at[kind, lane, way], recv_sem.at[kind, origin], dev)
        if when is None:
            copy.start()
        else:
            pl.when(when)(copy.start)
        return copy, when

    def wait(kind, origin):
        dst = place(kind, origin)
        remote(dst, dst, send_sem.at[kind, 0, 0], recv_sem.at[kind, origin], at.twin).wait_recv()

    def finish(copy, when):
        if when is None:
            copy.wait_send()
        else:
            pl.when(when)(copy.wait_send)

    for kind in (0, 1, 2, 3, 4):
        started.append(send(kind, at.me, True, 0, at.up, at.has_up))
        started.append(send(kind, at.me, True, 1, at.down, at.has_down))
        started.append(send(kind, at.me, True, 2, at.side, None))
        started.append(send(kind, at.me, True, 3, at.twin, None))
    wait(0, at.side)
    started.append(send(0, at.side, False, 0, at.up, at.has_up))
    started.append(send(0, at.side, False, 1, at.down, at.has_down))
    started.append(send(0, at.side, False, 3, at.twin, None))
    tails = []

    for hop in (1, 2, 3):
        for kind, swap in ((0, False), (1, False), (2, False), (0, True), (3, False), (4, False)):
            for sign in (-1, 1):
                far = at.z + sign * hop
                there = (far >= 0) & (far < 4)
                origin = (at.side if swap else at.me) + 4 * sign * hop

                def relay(kind=kind, origin=origin, sign=sign):
                    wait(kind, origin)
                    if sign < 0:
                        send(kind, origin, False, 0, at.up, at.has_up)
                    else:
                        send(kind, origin, False, 1, at.down, at.has_down)
                    if kind > 0:
                        send(kind, origin, False, 2, at.side, None)
                    send(kind, origin, False, 3, at.twin, None)

                def ended(kind=kind, origin=origin, sign=sign):
                    def gone(way, dev):
                        src = place(kind, origin)
                        lane = lax.div(origin, 2)
                        return remote(src, src, send_sem.at[kind, lane, way], recv_sem.at[kind, origin], dev).wait_send

                    if sign < 0:
                        pl.when(at.has_up)(gone(0, at.up))
                    else:
                        pl.when(at.has_down)(gone(1, at.down))
                    if kind > 0:
                        gone(2, at.side)()
                    gone(3, at.twin)()

                pl.when(there)(relay)
                tails.append((there, ended))
        for sign in (-1, 1) if hop > 1 else (0,):
            far = at.z + sign * (hop - 1)
            side_block(at, wait, send, started, tails, far, at.side + 4 * sign * (hop - 1), place, send_sem, recv_sem)
    for sign in (-1, 1):
        side_block(at, wait, send, started, tails, at.z + sign * 3, at.side + 12 * sign, place, send_sem, recv_sem)
    for copy, when in started:
        finish(copy, when)
    for there, ended in tails:
        pl.when(there)(ended)
    for k in range(8):
        for kind in range(5):
            wait(kind, 2 * k + 1 - at.c)
    own_v.wait()
    own_o.wait()


def side_block(at, wait, send, started, tails, far, origin, place, send_sem, recv_sem):
    there = (far >= 0) & (far < 4)

    def relay():
        for kind in (1, 2, 3, 4):
            wait(kind, origin)
            send(kind, origin, False, 3, at.twin, None)

    def ended():
        for kind in (1, 2, 3, 4):
            src = place(kind, origin)
            lane = lax.div(origin, 2)
            remote(src, src, send_sem.at[kind, lane, 3], recv_sem.at[kind, origin], at.twin).wait_send()

    pl.when(there)(relay)
    tails.append((there, ended))


def gather_blocks(value_blocks, output_blocks):
    count = lax.axis_size("dp")
    if not own_plan():
        return tuple(lax.all_gather(b, "dp", axis=0, tiled=True) for b in (value_blocks, output_blocks))
    any_space = pl.BlockSpec(memory_space=pl.ANY)

    def whole(b):
        return jax.ShapeDtypeStruct((b.shape[0] * count,) + b.shape[1:], b.dtype)

    return pl.pallas_call(
        gather_kernel,
        out_shape=(whole(value_blocks), whole(output_blocks)),
        in_specs=[any_space] * 2,
        out_specs=(any_space,) * 2,
        scratch_shapes=[
            pltpu.SemaphoreType.DMA((5, 8, 4)),
            pltpu.SemaphoreType.DMA((5, 16)),
            pltpu.SemaphoreType.DMA((2,)),
        ],
        compiler_params=pltpu.CompilerParams(collective_id=0, has_side_effects=True),
        name="gather_blocks",
    )(value_blocks, output_blocks)


def layers_kernel(rows, heads, live, wv_in, we_in, x, g, gain, out, grad, vgrad, *scratch):
    got, ebf, u, ut, e32, g1, dv, dvb, v, part, got1, sum1, send2, got2, send3, got3, swap_sem, send_sem, recv_sem, wv, we, load_sem = scratch
    load_v = pltpu.make_async_copy(wv_in, wv, load_sem.at[0])
    load_o = pltpu.make_async_copy(we_in, we, load_sem.at[1])
    load_v.start()
    load_o.start()
    at = Links()
    section = lax.axis_index("section")
    barrier = pltpu.get_barrier_semaphore()
    pl.semaphore_signal(
        barrier, inc=1, device_id={"section": 1 - section}, device_id_type=pl.DeviceIdType.MESH
    )
    at.greet(False)
    width = x.shape[1]
    chips, cores, n, blk, _ = part.shape
    chunk = 512
    chunks = width // chunk

    def swap(src, i):
        cols = tile(i, chunk)
        return pltpu.make_async_remote_copy(
            src_ref=src.at[:, cols],
            dst_ref=got.at[:, cols],
            send_sem=swap_sem.at[0, i],
            recv_sem=swap_sem.at[1, i],
            device_id={"section": 1 - section},
            device_id_type=pl.DeviceIdType.MESH,
        )

    @pl.when(section == 0)
    def _():
        norm(x, gain, u)
        load_v.wait()
        forward_values(u, wv, v)
        load_o.wait()

        def mixed(i):
            cols = tile(i, chunk)
            m = dot(v[...], we[:, cols], NN)
            out[:, cols] = (x[:, cols].astype(F32) + m).astype(BF)
            swap(out, i).start()

        loop(chunks, mixed)
        flip(u, ut)

    @pl.when(section == 1)
    def _():
        load_o.wait()
        backward_values(g, we, dv)
        load_v.wait()

        def gained(i):
            cols = tile(i, chunk)
            e = dot(dv[...], wv[cols, :], NT) * gain[:, cols].astype(F32)
            e32[:, cols] = e
            ebf[:, cols] = e.astype(BF)
            swap(ebf, i).start()

        loop(chunks, gained)

    loop(chunks, lambda i: swap(ebf, i).wait_recv())

    @pl.when(section == 0)
    def _():
        backward_norm(g, out, got, g1)
        backward_values(g1, we, dv)

    @pl.when(section == 1)
    def _():
        norm(got, gain, u)
        flip(u, ut)

    def by_head(h):
        dvb[h] = dv[:, tile(h, blk)]

    loop(dvb.shape[0], by_head)

    def slots(k, core):
        for i in range(n):
            j = (k * 2 + core) * n + i
            part[k, core, i] = dot(ut[rows[j]], dvb[heads[j]], NN) * live[j]

    def to_twin(k):
        return remote(part.at[k, 1 - at.c], got1.at[k], send_sem.at[k], recv_sem.at[k], at.twin)

    def for_twin(k):
        slots(k, 1 - at.c)
        to_twin(k).start()

    loop(chips, for_twin)
    loop(chips, lambda k: slots(k, at.c))
    second = []
    for z in range(4):
        for k in (2 * z, 2 * z + 1):
            to_twin(k).wait_recv()
            sum1[k] = part[k, at.c] + got1[k]
        send2[z] = sum1[2 * z + 1 - at.y].astype(BF)
        copy = remote(send2.at[z], got2.at[z], send_sem.at[8 + z], recv_sem.at[8 + z], at.side)
        copy.start()
        second.append(copy)

    @pl.when(section == 0)
    def _():
        backward_gained(dv, wv, gain, (e32,))

    @pl.when(section == 1)
    def _():
        backward_norm(g, got, e32, grad)
        forward_values(u, wv, v)

    for z in range(4):
        second[z].wait_recv()
        k = 2 * z + at.y
        total = sum1[k] + got2[z].astype(F32)
        sum1[k] = total
        send3[z] = total.astype(BF)

        @pl.when(at.z != z)
        def _():
            remote(
                send3.at[z], got3.at[at.z], send_sem.at[12 + z], recv_sem.at[12 + at.z], z * 4 + lax.rem(at.me, 4)
            ).start()

    @pl.when(section == 0)
    def _():
        backward_norm(g1, x, e32, grad)

    @pl.when(section == 1)
    def _():
        forward_mixed(got, v, we, out)

    vgrad[...] = sum1[2 * at.z + at.y]
    for z in range(4):

        @pl.when(at.z != z)
        def _():
            copy = remote(
                send3.at[z], got3.at[z], send_sem.at[12 + z], recv_sem.at[12 + z], z * 4 + lax.rem(at.me, 4)
            )
            copy.wait_recv()
            copy.wait_send()
            vgrad[...] += got3[z].astype(F32)

    for copy in second:
        copy.wait_send()
    loop(chips, lambda k: to_twin(k).wait_send())
    loop(chunks, lambda i: swap(ebf, i).wait_send())


def two_sections(meta, vidx, oidx, vp, op, x, g, gain):
    tokens, width = x.shape
    slots, blk, _ = vp.shape
    n = slots // lax.axis_size("dp")
    wide = jax.ShapeDtypeStruct((tokens, width), BF)
    heads = KVW // blk
    live = (jnp.arange(slots) < meta[1]).astype(F32) / tokens
    wv, we = dense_weights(meta, vidx, oidx, vp, op, width)
    return pl.pallas_call(
        layers_kernel,
        out_shape=(wide, wide, jax.ShapeDtypeStruct((n, blk, blk), F32)),
        in_specs=[SMEM] * 3 + [pl.BlockSpec(memory_space=pl.ANY)] * 2 + [VMEM] * 3,
        out_specs=(VMEM,) * 3,
        scratch_shapes=[
            pltpu.VMEM((tokens, width), BF),
            pltpu.VMEM((tokens, width), BF),
            pltpu.VMEM((tokens, width), BF),
            pltpu.VMEM((width // blk, blk, tokens), BF),
            pltpu.VMEM((tokens, width), F32),
            pltpu.VMEM((tokens, width), BF),
            pltpu.VMEM((tokens, KVW), BF),
            pltpu.VMEM((KVW // blk, tokens, blk), BF),
            pltpu.VMEM((tokens, KVW), BF),
            pltpu.VMEM((8, 2, n, blk, blk), F32),
            pltpu.VMEM((8, n, blk, blk), F32),
            pltpu.VMEM((8, n, blk, blk), F32),
            pltpu.VMEM((4, n, blk, blk), BF),
            pltpu.VMEM((4, n, blk, blk), BF),
            pltpu.VMEM((4, n, blk, blk), BF),
            pltpu.VMEM((4, n, blk, blk), BF),
            pltpu.SemaphoreType.DMA((2, width // 512)),
            pltpu.SemaphoreType.DMA((16,)),
            pltpu.SemaphoreType.DMA((16,)),
            pltpu.VMEM((width, KVW), BF),
            pltpu.VMEM((KVW, width), BF),
            pltpu.SemaphoreType.DMA((2,)),
        ],
        compiler_params=pltpu.CompilerParams(collective_id=1, has_side_effects=True, vmem_limit_bytes=60 << 20),
        name="layers",
    )(vidx[0] // heads, vidx[0] % heads, live, wv, we, x, g, gain)


def dense_weights(meta, vidx, oidx, vp, op, width):
    return pl.pallas_call(
        build_dense,
        out_shape=(jax.ShapeDtypeStruct((width, KVW), BF), jax.ShapeDtypeStruct((KVW, width), BF)),
        in_specs=[SMEM] * 3 + [pl.BlockSpec(memory_space=pl.ANY)] * 2,
        out_specs=(pl.BlockSpec(memory_space=pl.ANY),) * 2,
        scratch_shapes=[
            pltpu.VMEM(vp.shape, BF),
            pltpu.VMEM(op.shape, BF),
            pltpu.VMEM((width, KVW), BF),
            pltpu.VMEM((KVW, width), BF),
            pltpu.VMEM((KVW, width), F32),
            pltpu.SemaphoreType.DMA((3 + KVW // vp.shape[-1],)),
        ],
        compiler_params=params(),
        name="build_dense",
    )(meta, vidx, oidx, vp, op)


def many_sections(meta, vidx, oidx, vp, op, x, g, gain):
    sections = lax.axis_size("section")
    here = meta[0]
    tokens, width = x.shape
    slots, blk, _ = vp.shape
    wv, we = dense_weights(meta, vidx, oidx, vp, op, width)
    gain_row = gain.astype(F32)

    def scale(a):
        return lax.rsqrt(jnp.mean(a * a, axis=-1, keepdims=True) + EPS)

    def layer(cur):
        a = cur.astype(F32)
        u = (a * scale(a) * gain_row).astype(BF)
        v = dot(u, wv, NN).astype(BF)
        return (a + dot(v, we, NN)).astype(BF), u

    def fwd(t, cur):
        got = lax.ppermute(layer(cur)[0], "section", [(i, i + 1) for i in range(sections - 1)])
        return jnp.where(here == t + 1, got, cur)

    cur = lax.fori_loop(0, sections - 1, fwd, x)
    out, u = layer(cur)
    a = cur.astype(F32)
    r = scale(a)

    def back(gin):
        dv = dot(gin, we, NT).astype(BF)
        e = dot(dv, wv, NT) * gain_row
        m = jnp.mean(e * a, axis=-1, keepdims=True)
        return (gin.astype(F32) + r * e - r * r * r * a * m).astype(BF), dv

    def bwd(t, gin):
        got = lax.ppermute(back(gin)[0], "section", [(i + 1, i) for i in range(sections - 1)])
        return jnp.where(here == sections - 2 - t, got, gin)

    gin = lax.fori_loop(0, sections - 1, bwd, g)
    grad, dv = back(gin)
    heads = KVW // blk
    picked_in = jnp.take(u.reshape(tokens, -1, blk), vidx[0] // heads, axis=1)
    picked_out = jnp.take(dv.reshape(tokens, heads, blk), vidx[0] % heads, axis=1)
    part = jnp.einsum("tgk,tgn->gkn", picked_in, picked_out, preferred_element_type=F32)
    live = (jnp.arange(slots) < meta[1]).astype(F32) / tokens
    part = part * live[:, None, None]
    return out, grad, lax.psum_scatter(part, "dp", scatter_dimension=0, tiled=True)


def on_device(x, g, gain, value_blocks, output_blocks, vidx, oidx, vcount, ocount):
    here = lax.axis_index("section").astype(jnp.int32)
    vp, op = gather_blocks(value_blocks[0], output_blocks[0])
    meta = jnp.stack([here, vcount[0], ocount[0]])
    run = two_sections if own_plan() else many_sections
    out, grad, vgrad = run(meta, vidx, oidx, vp, op, x, g, gain)
    return out[None], grad[None], vgrad[None]


def solution(mesh):
    return jax.shard_map(
        on_device,
        mesh=mesh,
        in_specs=(
            P("dp", None),
            P("dp", None),
            P("section", None),
            P("section", "dp", None, None),
            P("section", "dp", None, None),
            P("section", None),
            P("section", None),
            P("section"),
            P("section"),
        ),
        out_specs=(
            P("section", "dp", None),
            P("section", "dp", None),
            P("section", "dp", None, None),
        ),
        check_vma=False,
    )
```
